128 devices in a mesh: wide: 16 (over z_hi, x, core), narrow: 8 (over z_lo, y).
Axes of the slice: x: 4, y: 4, z: 4 (z_hi: 2, z_lo: 2; z = z_hi * 2 + z_lo), core: 2. Of those that a mesh axis runs over, the one named last changes fastest.
Arguments:
- slope_first: float32 [768, 768, 256], P('wide', 'narrow'), may hold values from -3.1416 to 3.1416, as said below
- slope_second: float32 [768, 768, 256], P('wide', 'narrow'), may hold values from -3.1416 to 3.1416, as said below
- slope_third: float32 [768, 768, 256], P('wide', 'narrow'), may hold values from -3.1416 to 3.1416, as said below
Outputs:
- unwrapped_phase: float32 [768, 768, 256], P('wide', 'narrow')
The draws below stay inside these ranges and needn't reach their ends.
Inputs may be any that keep to these rules, and one draw needn't show every extreme that they name: `slope_first`: wrapped phase differences. `slope_second`: wrapped phase differences. `slope_third`: wrapped phase differences.
All inputs are finite; a program needn't handle non-finite values.
Results may differ from the reference program's by a relative error of at most 0.0003.
Values sent between devices are 32-bit elements; how exact they have to be, the bound alone decides.
A program may use at most 128 MiB of HBM per device.

```python
import math
import jax
import jax.numpy as jnp
from jax import lax

NX = 768
NY = 768
NZ = 256


def field_draw(key, salt):
    keys = jax.random.split(jax.random.fold_in(key, salt), 1)
    shape = (NX, NY, NZ)
    value = jax.random.normal(keys[0], shape, dtype=jnp.float32) * 0.9
    return jnp.clip(value, -3.0, 3.0).astype(jnp.float32)


def draw_slope_first(key, part):
    return field_draw(key, 11)


def draw_slope_second(key, part):
    return field_draw(key, 23)


def draw_slope_third(key, part):
    return field_draw(key, 37)


def setup_inputs(seed: int = 0) -> dict:
    key_of = jax.random.split(jax.random.key(seed), 4)
    return {
        "slope_first": draw_slope_first(jax.random.fold_in(key_of[3], 71), 0),
        "slope_second": draw_slope_second(jax.random.fold_in(key_of[3], 71), 0),
        "slope_third": draw_slope_third(jax.random.fold_in(key_of[3], 71), 0),
    }


def cosine_table(length, columns):
    rows = jnp.arange(length, dtype=jnp.int32)[:, None]
    phase = (2 * columns[None, :] + 1) * rows % (4 * length)
    angle = phase.astype(jnp.float32) * (math.pi / (2 * length))
    weight = jnp.where(rows == 0, math.sqrt(1.0 / length), math.sqrt(2.0 / length))
    return (weight * jnp.cos(angle)).astype(jnp.float32)

def eigen_part(count, index):
    half_sine = jnp.sin(index.astype(jnp.float32) * (math.pi / (2 * count)))
    return -4.0 * half_sine * half_sine

def reference(slope_first, slope_second, slope_third):
    size_first, size_second, size_third = slope_first.shape
    index_first = jnp.arange(size_first, dtype=jnp.int32)
    index_second = jnp.arange(size_second, dtype=jnp.int32)
    index_third = jnp.arange(size_third, dtype=jnp.int32)
    flux_first = jnp.where((index_first < size_first - 1)[:, None, None], slope_first, jnp.float32(0.0))
    flux_second = jnp.where((index_second < size_second - 1)[None, :, None], slope_second, jnp.float32(0.0))
    flux_third = jnp.where((index_third < size_third - 1)[None, None, :], slope_third, jnp.float32(0.0))
    zero_plane = jnp.zeros((1, size_second, size_third), jnp.float32)
    zero_row = jnp.zeros((size_first, 1, size_third), jnp.float32)
    zero_line = jnp.zeros((size_first, size_second, 1), jnp.float32)
    source = flux_first - jnp.concatenate([zero_plane, flux_first[:-1]], axis=0)
    source = source + flux_second - jnp.concatenate([zero_row, flux_second[:, :-1]], axis=1)
    source = source + flux_third - jnp.concatenate([zero_line, flux_third[:, :, :-1]], axis=2)
    depth_table = cosine_table(size_third, index_third)
    row_table = cosine_table(size_second, index_second)
    column_table = cosine_table(size_first, index_first)
    highest = lax.Precision.HIGHEST
    spectrum = jnp.einsum('abn,kn->abk', source, depth_table, precision=highest)
    spectrum = jnp.einsum('anc,kn->akc', spectrum, row_table, precision=highest)
    spectrum = jnp.einsum('xbc,kx->kbc', spectrum, column_table, precision=highest)
    eigenvalue = eigen_part(size_first, index_first)[:, None, None] + eigen_part(size_second, index_second)[None, :, None] + eigen_part(size_third, index_third)[None, None, :]
    zero_mode = (index_first == 0)[:, None, None] & (index_second == 0)[None, :, None] & (index_third == 0)[None, None, :]
    solved = jnp.where(zero_mode, jnp.float32(0.0), spectrum / jnp.where(zero_mode, jnp.float32(1.0), eigenvalue))
    result = jnp.einsum('kbc,kx->xbc', solved, column_table, precision=highest)
    result = jnp.einsum('akc,kn->anc', result, row_table, precision=highest)
    result = jnp.einsum('abk,kn->abn', result, depth_table, precision=highest)
    return result
```

```python
import functools
import math

import jax
import jax.numpy as jnp
import numpy as np
from jax import lax
from jax.experimental import pallas as pl
from jax.experimental.pallas import tpu as pltpu
from jax.sharding import PartitionSpec as P

HIGHEST = lax.Precision.HIGHEST


LANES = 128


def cosine_matrix(length):
    k = np.arange(length)[:, None]
    n = np.arange(length)[None, :]
    table = np.sqrt(2.0 / length) * np.cos(np.pi * ((2 * n + 1) * k % (4 * length)) / (2 * length))
    table[0] = np.sqrt(1.0 / length)
    return table


def sine_matrix(parts):
    m = np.arange(1, parts)
    return np.sqrt(2.0 / parts) * np.sin(np.pi * m[:, None] * m[None, :] / parts)


def modes(length):
    return 4.0 * np.sin(np.pi * np.arange(length) / (2 * length)) ** 2


def signs(length):
    return (-1.0) ** np.arange(length)


def face(length):
    return cosine_matrix(length)[:, 0]


def exponent(mu):
    return 2.0 * np.arcsinh(np.sqrt(mu) / 2.0)


def interface_gain(mu, cells, parts):
    kappa = exponent(mu)[..., None]
    angle = np.pi * np.arange(1, parts) / parts
    decay = np.exp(-kappa * cells)
    ratio = -np.expm1(-2.0 * kappa * cells) / (np.expm1(-kappa * cells) ** 2 + 2.0 * decay * (1.0 - np.cos(angle)))
    return np.tanh(kappa / 2.0) * ratio


def running_levels(parts):
    part = np.arange(parts)[:, None]
    step = np.arange(1, parts)[None, :]
    return (step <= part) - (parts - step) / parts


@functools.lru_cache(None)
def tables(rows, lines, depth, wide, narrow):
    t = {}
    row_modes, line_modes, depth_modes = modes(rows), modes(lines), modes(depth)
    row_face, line_face = face(rows), face(lines)
    sine_n = sine_matrix(narrow)
    gain = interface_gain(depth_modes[:, None] + row_modes[None, :], lines, narrow)
    gain[0, 0, :] = 0.0
    t["narrow_gain"] = np.swapaxes(gain, 1, 2)
    t["narrow_sines"] = np.einsum("jm,ml->mjl", sine_n, sine_n)
    levels_n = running_levels(narrow)
    t["narrow_steady"] = np.cumsum(-levels_n / line_face[0], axis=0)[:-1] / line_face[0]
    full = cosine_matrix(lines * narrow)
    local = cosine_matrix(lines)
    t["join"] = np.einsum("qJn,kn->qJk", full.reshape(lines * narrow, narrow, lines), local).reshape(
        lines * narrow, lines * narrow
    )
    t["wide_decay"] = np.expm1(-exponent(depth_modes[:, None] + modes(lines * narrow)[None, :]) * rows)
    t["wide_sine"] = sine_matrix(wide)
    t["wide_angle"] = 1.0 - np.cos(np.pi * np.arange(1, wide) / wide)
    t["wide_levels"] = -running_levels(wide) / (row_face[0] * math.sqrt(narrow))
    balance = -(row_face[0] / line_face[0]) * np.tril(np.ones((narrow - 1, narrow)))
    t["balance"] = balance.T
    k = np.arange(1, lines)
    near = np.sum(line_face[k] ** 2 / line_modes[k])
    far = np.sum(signs(lines)[k] * line_face[k] ** 2 / line_modes[k])
    link = (1.0 + 2.0 * near) * np.eye(narrow - 1) - far * (np.eye(narrow - 1, k=1) + np.eye(narrow - 1, k=-1))
    t["level_of_flux"] = (levels_n @ link / line_face[0]).T
    t["level_of_jump"] = (-levels_n / line_face[0]).T
    return {name: np.ascontiguousarray(value, dtype=np.float32) for name, value in t.items()}


def halves(table):
    table = np.asarray(table, np.float32)
    high = table.astype(jnp.bfloat16)
    low = (table - high.astype(np.float32)).astype(jnp.bfloat16)
    return high, low


def left_table(table):
    high, low = halves(table)
    return np.block([[high, high], [low, np.zeros_like(low)]])


def split(x):
    high = x.astype(jnp.bfloat16)
    return high, (x - high.astype(jnp.float32)).astype(jnp.bfloat16)


def dot(a, b):
    return jnp.dot(a, b, preferred_element_type=jnp.float32)


def from_left(table, x):
    both = dot(table, jnp.concatenate(split(x), axis=0))
    count = x.shape[0]
    return both[:count] + both[count:]


def from_right(x, high_table, low_table):
    high, low = split(x)
    return dot(high, high_table) + dot(low, high_table) + dot(high, low_table)


def lower_neighbour(x, axis):
    index = lax.broadcasted_iota(jnp.int32, x.shape, axis)
    x = jnp.where(index < x.shape[axis] - 1, x, 0.0)
    return pltpu.roll(x, 1, axis) - x


def put(held, where, value):
    for panel in range(held.shape[0]):
        held[panel, where, :] = value[:, panel * LANES : (panel + 1) * LANES]


def take(held, where):
    return jnp.concatenate([held[panel, where, :] for panel in range(held.shape[0])], axis=1)


def forward_kernel(
    steps,
    first_ref,
    second_ref,
    third_ref,
    depth_high_ref,
    depth_low_ref,
    line_ref,
    row_ref,
    shift_ref,
    faces_ref,
    line_shift_ref,
    line_face_ref,
    out_ref,
    wide_ref,
    narrow_ref,
    carry,
    held,
):
    step = pl.program_id(0)
    rows, lines = row_ref.shape[0] // 2, line_ref.shape[0] // 2
    block = first_ref.shape[0]
    group = out_ref.shape[0]

    @pl.when(step == 0)
    def _():
        carry[...] = jnp.zeros_like(carry)
        narrow_ref[...] = jnp.zeros_like(narrow_ref)

    @pl.when(step < steps)
    def _():
        below = carry[...]
        parts = []
        for i in range(block):
            here = first_ref[i]
            if i == block - 1:
                here = jnp.where(step < steps - 1, here, 0.0)
            part = below - here + lower_neighbour(second_ref[i], 0) + lower_neighbour(third_ref[i], 1)
            below = here
            parts.append(part)
        carry[...] = below
        stacked = from_right(jnp.concatenate(parts, axis=0), depth_high_ref[...], depth_low_ref[...])
        for i in range(block):
            part = from_left(line_ref[...], stacked[i * lines : (i + 1) * lines])
            put(held, pl.ds(pl.multiple_of((step * block + i) * lines, 8), lines), part)

    @pl.when(step >= steps)
    def _():
        lows, highs = [], []
        narrow_low, narrow_high = narrow_ref[0], narrow_ref[1]
        for i in range(group):
            line = (step - steps) * group + i
            part = from_left(row_ref[...], take(held, pl.ds(line, rows, stride=lines)))
            out_ref[i] = part
            eig = shift_ref[...] + line_shift_ref[line]
            good = eig > 0.0
            closed = jnp.where(good, part / jnp.where(good, eig, 1.0), 0.0)
            lows.append(jnp.sum(closed * faces_ref[0], axis=0, keepdims=True))
            highs.append(jnp.sum(closed * faces_ref[1], axis=0, keepdims=True))
            closed = closed * line_face_ref[line]
            narrow_low = narrow_low + closed
            narrow_high = narrow_high + closed if i % 2 == 0 else narrow_high - closed
        wide_ref[0] = jnp.concatenate(lows, axis=0)
        wide_ref[1] = jnp.concatenate(highs, axis=0)
        narrow_ref[0] = narrow_low
        narrow_ref[1] = narrow_high


def inverse_kernel(
    steps,
    spectrum_ref,
    wide_ref,
    narrow_ref,
    level_ref,
    depth_high_ref,
    depth_low_ref,
    line_ref,
    row_ref,
    shift_ref,
    faces_ref,
    line_shift_ref,
    line_face_ref,
    out_ref,
    held,
):
    step = pl.program_id(0)
    rows, lines = row_ref.shape[0] // 2, line_ref.shape[0] // 2
    block = out_ref.shape[0]
    group = spectrum_ref.shape[0]

    @pl.when(step < steps)
    def _():
        for i in range(group):
            line = step * group + i
            added = faces_ref[1] * wide_ref[1, i : i + 1, :] - faces_ref[0] * wide_ref[0, i : i + 1, :]
            turned = narrow_ref[1] if i % 2 == 0 else -narrow_ref[1]
            part = spectrum_ref[i] + added + line_face_ref[line] * (turned - narrow_ref[0])
            eig = shift_ref[...] + line_shift_ref[line]
            good = eig > 0.0
            part = jnp.where(good, part / jnp.where(good, eig, 1.0), level_ref[...])
            put(held, pl.ds(line, rows, stride=lines), from_left(row_ref[...], part))

    @pl.when(step >= steps)
    def _():
        parts = []
        for i in range(block):
            here = pl.multiple_of(((step - steps) * block + i) * lines, 8)
            parts.append(from_left(line_ref[...], take(held, pl.ds(here, lines))))
        result = from_right(jnp.concatenate(parts, axis=0), depth_high_ref[...], depth_low_ref[...])
        for i in range(block):
            out_ref[i] = result[i * lines : (i + 1) * lines]


BLOCK = 4
GROUP = 8


def box_tables(rows, lines, depth):
    shift = modes(rows)[:, None] + modes(depth)[None, :]
    low = np.broadcast_to(face(rows)[:, None], (rows, depth))
    high = np.broadcast_to((face(rows) * signs(rows))[:, None], (rows, depth))
    faces = np.stack([low, high])
    return [jnp.asarray(v, jnp.float32) for v in (shift, faces, modes(lines), face(lines))]


def whole(*shape):
    return pl.BlockSpec(shape, lambda s: (0,) * len(shape))


def table_specs(rows, lines, depth):
    return [
        whole(depth, depth),
        whole(depth, depth),
        whole(2 * lines, 2 * lines),
        whole(2 * rows, 2 * rows),
        whole(rows, depth),
        whole(2, rows, depth),
        pl.BlockSpec(memory_space=pltpu.SMEM),
        pl.BlockSpec(memory_space=pltpu.SMEM),
    ]


def forward(first, second, third):
    rows, lines, depth = first.shape
    steps, groups = rows // BLOCK, lines // GROUP
    slab = pl.BlockSpec((BLOCK, lines, depth), lambda s: (jnp.minimum(s, steps - 1), 0, 0))
    depth_high, depth_low = halves(cosine_matrix(depth).T)
    f32 = jnp.float32
    return pl.pallas_call(
        functools.partial(forward_kernel, steps),
        grid=(steps + groups,),
        out_shape=[
            jax.ShapeDtypeStruct((lines, rows, depth), f32),
            jax.ShapeDtypeStruct((2, lines, depth), f32),
            jax.ShapeDtypeStruct((2, rows, depth), f32),
        ],
        in_specs=[slab, slab, slab] + table_specs(rows, lines, depth),
        out_specs=[
            pl.BlockSpec((GROUP, rows, depth), lambda s: (jnp.maximum(s - steps, 0), 0, 0)),
            pl.BlockSpec((2, GROUP, depth), lambda s: (0, jnp.maximum(s - steps, 0), 0)),
            whole(2, rows, depth),
        ],
        scratch_shapes=[pltpu.VMEM((lines, depth), f32), pltpu.VMEM((depth // LANES, rows * lines, LANES), f32)],
        compiler_params=pltpu.CompilerParams(vmem_limit_bytes=48 * 2**20),
    )(
        first,
        second,
        third,
        jnp.asarray(depth_high),
        jnp.asarray(depth_low),
        jnp.asarray(left_table(cosine_matrix(lines))),
        jnp.asarray(left_table(cosine_matrix(rows))),
        *box_tables(rows, lines, depth),
    )


def inverse(spectrum, wide_flux, narrow_flux, level):
    lines, rows, depth = spectrum.shape
    steps, groups = rows // BLOCK, lines // GROUP
    depth_high, depth_low = halves(cosine_matrix(depth))
    return pl.pallas_call(
        functools.partial(inverse_kernel, groups),
        grid=(steps + groups,),
        out_shape=jax.ShapeDtypeStruct((rows, lines, depth), jnp.float32),
        in_specs=[
            pl.BlockSpec((GROUP, rows, depth), lambda s: (jnp.minimum(s, groups - 1), 0, 0)),
            pl.BlockSpec((2, GROUP, depth), lambda s: (0, jnp.minimum(s, groups - 1), 0)),
            whole(2, rows, depth),
            whole(1, depth),
        ]
        + table_specs(rows, lines, depth),
        out_specs=pl.BlockSpec((BLOCK, lines, depth), lambda s: (jnp.maximum(s - groups, 0), 0, 0)),
        scratch_shapes=[pltpu.VMEM((depth // LANES, rows * lines, LANES), jnp.float32)],
        compiler_params=pltpu.CompilerParams(vmem_limit_bytes=48 * 2**20),
    )(
        spectrum,
        wide_flux,
        narrow_flux,
        level,
        jnp.asarray(depth_high),
        jnp.asarray(depth_low),
        jnp.asarray(left_table(cosine_matrix(lines).T)),
        jnp.asarray(left_table(cosine_matrix(rows).T)),
        *box_tables(rows, lines, depth),
    )


def own(table, place, count):
    return lax.dynamic_slice_in_dim(jnp.asarray(table), place * count, count, axis=0)


def alternate(length):
    return jnp.asarray(signs(length), jnp.float32)


def eigen(index, count):
    half_sine = jnp.sin(index.astype(jnp.float32) * (math.pi / (2 * count)))
    return 4.0 * half_sine * half_sine


def interfaces(traces, t, place, rows, lines, depth, wide, narrow):
    count = traces.shape[1]
    traces = traces.reshape(wide, narrow, count, -1)
    traces = jnp.transpose(traces, (2, 0, 1, 3))
    cut = [lines, 2 * lines, 2 * lines + rows]
    wide_low, wide_high, narrow_low, narrow_high = jnp.split(traces, cut, axis=-1)
    jump_wide = wide_low[:, 1:] - wide_high[:, :-1]
    jump_narrow = narrow_low[:, :, 1:] - narrow_high[:, :, :-1]
    depth_place = place * count + jnp.arange(count)
    steady = depth_place == 0
    depth_part = eigen(depth_place, depth)
    row_zero = jnp.arange(rows) == 0
    line_zero = jnp.arange(lines) == 0
    last = jnp.einsum("mjl,rmk->rjlk", t["narrow_sines"], own(t["narrow_gain"], place, count), precision=HIGHEST)
    first = jnp.where(
        steady[:, None, None, None] & row_zero, jnp.asarray(t["narrow_steady"])[None, :, :, None], last
    )
    eig = (
        depth_part[:, None, None]
        + jnp.asarray(modes(rows), jnp.float32)[:, None]
        + jnp.asarray(modes(lines), jnp.float32)[None, :]
    )
    faces = jnp.asarray(face(rows)[:, None] * face(lines)[None, :], jnp.float32)
    steady_row = steady[:, None, None] & row_zero[:, None]
    zero_mode = steady_row & line_zero
    weight = faces / jnp.where(zero_mode, 1.0, eig)
    weight_first = jnp.where(steady_row & ~line_zero, 0.0, weight)
    weight_last = jnp.swapaxes(jnp.where(zero_mode, 0.0, weight), 1, 2)
    to_wide = jnp.stack([weight_first, weight_first * alternate(rows)[:, None]], axis=2)
    to_narrow = jnp.stack([weight_last, weight_last * alternate(lines)[:, None]], axis=2)
    shift = depth_part[:, None] + jnp.asarray(modes(lines * narrow), jnp.float32)[None, :]
    decay = own(t["wide_decay"], place, count)
    top = -jnp.sqrt(shift / (4.0 + shift)) * decay * (2.0 + decay)
    top = top[:, None, :]
    decay = decay[:, None, :]
    bottom = decay * decay + 2.0 * (1.0 + decay) * jnp.asarray(t["wide_angle"])[None, :, None]
    wide_gain = top / bottom
    flux = jnp.sum(first[:, None] * jump_narrow[:, :, None], axis=3)
    moved = jnp.einsum("rIjk,rksb->rsIjb", flux, to_wide, precision=HIGHEST)
    edge = [(0, 0)] * 3
    moved = jnp.pad(moved, edge + [(0, 1), (0, 0)]) * alternate(lines) - jnp.pad(moved, edge + [(1, 0), (0, 0)])
    jump_wide = jump_wide + moved[:, 0, 1:] - moved[:, 1, :-1]
    jump_wide = jump_wide.reshape(count, wide - 1, narrow * lines)
    joined = jnp.einsum("riy,qy->riq", jump_wide, t["join"], precision=HIGHEST)
    shaped = jnp.einsum("mi,riq->rmq", t["wide_sine"], joined, precision=HIGHEST)
    shaped = shaped * wide_gain
    shaped = jnp.einsum("mi,rmq->riq", t["wide_sine"], shaped, precision=HIGHEST)
    flux_wide = jnp.einsum("riq,qy->riy", shaped, t["join"], precision=HIGHEST)
    flux_wide = flux_wide.reshape(count, wide - 1, narrow, lines)
    flux_wide = jnp.pad(flux_wide, [(0, 0), (1, 1), (0, 0), (0, 0)])
    moved = jnp.einsum("riJb,rbsk->rsiJk", flux_wide, to_narrow, precision=HIGHEST)
    moved = moved[:, :, 1:] * alternate(rows) - moved[:, :, :-1]
    jump_narrow = jump_narrow + moved[:, 0, :, 1:] - moved[:, 1, :, :-1]
    flux_narrow = jnp.sum(last[:, None] * jump_narrow[:, :, None], axis=3)
    mean_flux = flux_wide[0, 1:, :, 0] - flux_wide[0, :-1, :, 0]
    balanced = jnp.einsum("IJ,Jj->Ij", mean_flux, t["balance"], precision=HIGHEST)
    level = jnp.einsum("Ij,jJ->IJ", balanced, t["level_of_flux"], precision=HIGHEST)
    level = level + jnp.einsum("Ij,jJ->IJ", jump_narrow[0, :, :, 0], t["level_of_jump"], precision=HIGHEST)
    level = level + jnp.einsum("Ii,i->I", t["wide_levels"], joined[0, :, 0], precision=HIGHEST)[:, None]
    flux_narrow = jnp.where(
        steady[:, None, None, None] & row_zero, balanced[None, :, :, None], flux_narrow
    )
    flux_narrow = jnp.pad(flux_narrow, [(0, 0), (0, 0), (1, 1), (0, 0)])
    level = jnp.broadcast_to(level[None, :, :, None], (count, wide, narrow, 8))
    out = jnp.concatenate(
        [flux_wide[:, :-1], flux_wide[:, 1:], flux_narrow[:, :, :-1], flux_narrow[:, :, 1:], level], axis=-1
    )
    out = jnp.transpose(out, (1, 2, 0, 3))
    return out.reshape(wide * narrow, count, -1)


def shards(slope_first, slope_second, slope_third):
    rows, lines, depth = slope_first.shape
    wide = lax.axis_size("wide")
    narrow = lax.axis_size("narrow")
    wide_place = lax.axis_index("wide")
    narrow_place = lax.axis_index("narrow")
    place = wide_place * narrow + narrow_place
    devices = wide * narrow
    t = tables(rows, lines, depth, wide, narrow)
    row_table = jnp.asarray(cosine_matrix(rows), jnp.float32)
    line_table = jnp.asarray(cosine_matrix(lines), jnp.float32)
    depth_table = jnp.asarray(cosine_matrix(depth), jnp.float32)
    spectrum, wide_traces, narrow_traces = forward(slope_first, slope_second, slope_third)
    slope_wide = jnp.einsum("yz,rz->yr", slope_first[-1], depth_table, precision=HIGHEST)
    slope_wide = jnp.einsum("yr,ky->kr", slope_wide, line_table, precision=HIGHEST)
    slope_narrow = jnp.einsum("xz,rz->xr", slope_second[:, -1], depth_table, precision=HIGHEST)
    slope_narrow = jnp.einsum("xr,kx->kr", slope_narrow, row_table, precision=HIGHEST)
    traces = jnp.concatenate(
        [wide_traces[0], wide_traces[1] + slope_wide, narrow_traces[0], narrow_traces[1] + slope_narrow], axis=0
    )
    traces = jnp.transpose(traces).reshape(devices, depth // devices, -1)
    traces = lax.all_to_all(traces, ("wide", "narrow"), split_axis=0, concat_axis=0, tiled=True)
    fluxes = interfaces(traces, t, place, rows, lines, depth, wide, narrow)
    fluxes = lax.all_to_all(fluxes, ("wide", "narrow"), split_axis=0, concat_axis=0, tiled=True)
    fluxes = jnp.transpose(fluxes.reshape(depth, -1))
    wide_flux = fluxes[: 2 * lines].reshape(2, lines, depth)
    narrow_flux = fluxes[2 * lines : 2 * (lines + rows)].reshape(2, rows, depth)
    level = fluxes[2 * (lines + rows) :][:1]
    return inverse(spectrum, wide_flux, narrow_flux, level)


def solution(mesh):
    placed = P("wide", "narrow", None)
    return jax.shard_map(shards, mesh=mesh, in_specs=(placed, placed, placed), out_specs=placed, check_vma=False)
```

```python
import functools
import math

import jax
import jax.numpy as jnp
import numpy as np
from jax import lax
from jax.experimental import pallas as pl
from jax.experimental.pallas import tpu as pltpu
from jax.sharding import PartitionSpec as P

HIGHEST = lax.Precision.HIGHEST


LANES = 128


def cosine_matrix(length):
    k = np.arange(length)[:, None]
    n = np.arange(length)[None, :]
    table = np.sqrt(2.0 / length) * np.cos(np.pi * ((2 * n + 1) * k % (4 * length)) / (2 * length))
    table[0] = np.sqrt(1.0 / length)
    return table


def sine_matrix(parts):
    m = np.arange(1, parts)
    return np.sqrt(2.0 / parts) * np.sin(np.pi * m[:, None] * m[None, :] / parts)


def modes(length):
    return 4.0 * np.sin(np.pi * np.arange(length) / (2 * length)) ** 2


def signs(length):
    return (-1.0) ** np.arange(length)


def face(length):
    return cosine_matrix(length)[:, 0]


def exponent(mu):
    return 2.0 * np.arcsinh(np.sqrt(mu) / 2.0)


def interface_gain(mu, cells, parts):
    kappa = exponent(mu)[..., None]
    angle = np.pi * np.arange(1, parts) / parts
    decay = np.exp(-kappa * cells)
    ratio = -np.expm1(-2.0 * kappa * cells) / (np.expm1(-kappa * cells) ** 2 + 2.0 * decay * (1.0 - np.cos(angle)))
    return np.tanh(kappa / 2.0) * ratio


def running_levels(parts):
    part = np.arange(parts)[:, None]
    step = np.arange(1, parts)[None, :]
    return (step <= part) - (parts - step) / parts


@functools.lru_cache(None)
def tables(rows, lines, depth, wide, narrow):
    t = {}
    row_modes, line_modes, depth_modes = modes(rows), modes(lines), modes(depth)
    row_face, line_face = face(rows), face(lines)
    sine_n = sine_matrix(narrow)
    gain = interface_gain(depth_modes[:, None] + row_modes[None, :], lines, narrow)
    gain[0, 0, :] = 0.0
    t["narrow_gain"] = np.swapaxes(gain, 1, 2)
    t["narrow_sines"] = np.einsum("jm,ml->mjl", sine_n, sine_n)
    levels_n = running_levels(narrow)
    t["narrow_steady"] = np.cumsum(-levels_n / line_face[0], axis=0)[:-1] / line_face[0]
    full = cosine_matrix(lines * narrow)
    local = cosine_matrix(lines)
    t["join"] = np.einsum("qJn,kn->qJk", full.reshape(lines * narrow, narrow, lines), local).reshape(
        lines * narrow, lines * narrow
    )
    t["wide_decay"] = np.expm1(-exponent(depth_modes[:, None] + modes(lines * narrow)[None, :]) * rows)
    t["wide_sine"] = sine_matrix(wide)
    t["wide_angle"] = 1.0 - np.cos(np.pi * np.arange(1, wide) / wide)
    t["wide_levels"] = -running_levels(wide) / (row_face[0] * math.sqrt(narrow))
    balance = -(row_face[0] / line_face[0]) * np.tril(np.ones((narrow - 1, narrow)))
    t["balance"] = balance.T
    k = np.arange(1, lines)
    near = np.sum(line_face[k] ** 2 / line_modes[k])
    far = np.sum(signs(lines)[k] * line_face[k] ** 2 / line_modes[k])
    link = (1.0 + 2.0 * near) * np.eye(narrow - 1) - far * (np.eye(narrow - 1, k=1) + np.eye(narrow - 1, k=-1))
    t["level_of_flux"] = (levels_n @ link / line_face[0]).T
    t["level_of_jump"] = (-levels_n / line_face[0]).T
    return {name: np.ascontiguousarray(value, dtype=np.float32) for name, value in t.items()}


def halves(table):
    table = np.asarray(table, np.float32)
    high = table.astype(jnp.bfloat16)
    low = (table - high.astype(np.float32)).astype(jnp.bfloat16)
    return high, low


def left_table(table):
    high, low = halves(table)
    return np.block([[high, high], [low, np.zeros_like(low)]])


def split(x):
    high = x.astype(jnp.bfloat16)
    return high, (x - high.astype(jnp.float32)).astype(jnp.bfloat16)


def dot(a, b):
    return jnp.dot(a, b, preferred_element_type=jnp.float32)


def from_left(table, x):
    both = dot(table, jnp.concatenate(split(x), axis=0))
    count = x.shape[0]
    return both[:count] + both[count:]


def from_right(x, high_table, low_table):
    high, low = split(x)
    return dot(high, high_table) + dot(low, high_table) + dot(high, low_table)


def lower_neighbour(x, axis):
    index = lax.broadcasted_iota(jnp.int32, x.shape, axis)
    x = jnp.where(index < x.shape[axis] - 1, x, 0.0)
    return pltpu.roll(x, 1, axis) - x


def put(held, where, value):
    for panel in range(held.shape[0]):
        held[panel, where, :] = value[:, panel * LANES : (panel + 1) * LANES]


def take(held, where):
    return jnp.concatenate([held[panel, where, :] for panel in range(held.shape[0])], axis=1)


def forward_kernel(
    steps,
    first_ref,
    second_ref,
    third_ref,
    depth_high_ref,
    depth_low_ref,
    line_ref,
    row_ref,
    shift_ref,
    faces_ref,
    line_shift_ref,
    line_face_ref,
    out_ref,
    wide_ref,
    narrow_ref,
    carry,
    held,
    wide_face,
    narrow_face,
):
    step = pl.program_id(0)
    rows, lines = row_ref.shape[0] // 2, line_ref.shape[0] // 2
    block = first_ref.shape[0]
    group = out_ref.shape[0]

    @pl.when(step == 0)
    def _():
        carry[...] = jnp.zeros_like(carry)

    @pl.when(step < steps)
    def _():
        below = carry[...]
        parts = []
        for i in range(block):
            here = first_ref[i]
            if i == block - 1:
                here = jnp.where(step < steps - 1, here, 0.0)
            part = below - here + lower_neighbour(second_ref[i], 0) + lower_neighbour(third_ref[i], 1)
            below = here
            parts.append(part)
            narrow_face[pl.ds(step * block + i, 1), :] = second_ref[i, lines - 1 : lines, :]
        carry[...] = below
        stacked = from_right(jnp.concatenate(parts, axis=0), depth_high_ref[...], depth_low_ref[...])
        for i in range(block):
            part = from_left(line_ref[...], stacked[i * lines : (i + 1) * lines])
            put(held, pl.ds(pl.multiple_of((step * block + i) * lines, 8), lines), part)

    @pl.when(step == steps)
    def _():
        face = from_right(first_ref[block - 1], depth_high_ref[...], depth_low_ref[...])
        wide_face[...] = from_left(line_ref[...], face)
        face = from_right(narrow_face[...], depth_high_ref[...], depth_low_ref[...])
        narrow_ref[0] = jnp.zeros_like(face)
        narrow_ref[1] = from_left(row_ref[...], face)

    @pl.when(step >= steps)
    def _():
        lows, highs = [], []
        narrow_low, narrow_high = narrow_ref[0], narrow_ref[1]
        for i in range(group):
            line = (step - steps) * group + i
            part = from_left(row_ref[...], take(held, pl.ds(line, rows, stride=lines)))
            out_ref[i] = part
            eig = shift_ref[...] + line_shift_ref[line]
            closed = jnp.where(eig > 0.0, part / eig, 0.0)
            lows.append(jnp.sum(closed * faces_ref[0], axis=0, keepdims=True))
            highs.append(jnp.sum(closed * faces_ref[1], axis=0, keepdims=True))
            closed = closed * line_face_ref[line]
            narrow_low = narrow_low + closed
            narrow_high = narrow_high + closed if i % 2 == 0 else narrow_high - closed
        wide_ref[0] = jnp.concatenate(lows, axis=0)
        here = pl.ds(pl.multiple_of((step - steps) * group, 8), group)
        wide_ref[1] = jnp.concatenate(highs, axis=0) + wide_face[here, :]
        narrow_ref[0] = narrow_low
        narrow_ref[1] = narrow_high


def inverse_kernel(
    steps,
    spectrum_ref,
    wide_ref,
    narrow_ref,
    level_ref,
    depth_high_ref,
    depth_low_ref,
    line_ref,
    row_ref,
    shift_ref,
    faces_ref,
    line_shift_ref,
    line_face_ref,
    out_ref,
    held,
):
    step = pl.program_id(0)
    rows, lines = row_ref.shape[0] // 2, line_ref.shape[0] // 2
    block = out_ref.shape[0]
    group = spectrum_ref.shape[0]

    @pl.when(step < steps)
    def _():
        for i in range(group):
            line = step * group + i
            added = faces_ref[1] * wide_ref[1, i : i + 1, :] - faces_ref[0] * wide_ref[0, i : i + 1, :]
            turned = narrow_ref[1] if i % 2 == 0 else -narrow_ref[1]
            part = spectrum_ref[i] + added + line_face_ref[line] * (turned - narrow_ref[0])
            eig = shift_ref[...] + line_shift_ref[line]
            part = jnp.where(eig > 0.0, part / eig, level_ref[...])
            put(held, pl.ds(line, rows, stride=lines), from_left(row_ref[...], part))

    @pl.when(step >= steps)
    def _():
        parts = []
        for i in range(block):
            here = pl.multiple_of(((step - steps) * block + i) * lines, 8)
            parts.append(from_left(line_ref[...], take(held, pl.ds(here, lines))))
        result = from_right(jnp.concatenate(parts, axis=0), depth_high_ref[...], depth_low_ref[...])
        for i in range(block):
            out_ref[i] = result[i * lines : (i + 1) * lines]


VMEM_LIMIT = 60 * 2**20
BLOCK = 16
GROUP = 16


def box_tables(rows, lines, depth):
    shift = modes(rows)[:, None] + modes(depth)[None, :]
    low = np.broadcast_to(face(rows)[:, None], (rows, depth))
    high = np.broadcast_to((face(rows) * signs(rows))[:, None], (rows, depth))
    faces = np.stack([low, high])
    return [jnp.asarray(v, jnp.float32) for v in (shift, faces, modes(lines), face(lines))]


def whole(*shape):
    return pl.BlockSpec(shape, lambda s: (0,) * len(shape))


def table_specs(rows, lines, depth):
    return [
        whole(depth, depth),
        whole(depth, depth),
        whole(2 * lines, 2 * lines),
        whole(2 * rows, 2 * rows),
        whole(rows, depth),
        whole(2, rows, depth),
        pl.BlockSpec(memory_space=pltpu.SMEM),
        pl.BlockSpec(memory_space=pltpu.SMEM),
    ]


def forward(first, second, third):
    rows, lines, depth = first.shape
    steps, groups = rows // BLOCK, lines // GROUP
    slab = pl.BlockSpec((BLOCK, lines, depth), lambda s: (jnp.minimum(s, steps - 1), 0, 0))
    depth_high, depth_low = halves(cosine_matrix(depth).T)
    f32 = jnp.float32
    return pl.pallas_call(
        functools.partial(forward_kernel, steps),
        grid=(steps + groups,),
        out_shape=[
            jax.ShapeDtypeStruct((lines, rows, depth), f32),
            jax.ShapeDtypeStruct((2, lines, depth), f32),
            jax.ShapeDtypeStruct((2, rows, depth), f32),
        ],
        in_specs=[slab, slab, slab] + table_specs(rows, lines, depth),
        out_specs=[
            pl.BlockSpec((GROUP, rows, depth), lambda s: (jnp.maximum(s - steps, 0), 0, 0)),
            pl.BlockSpec((2, GROUP, depth), lambda s: (0, jnp.maximum(s - steps, 0), 0)),
            whole(2, rows, depth),
        ],
        scratch_shapes=[
            pltpu.VMEM((lines, depth), f32),
            pltpu.VMEM((depth // LANES, rows * lines, LANES), f32),
            pltpu.VMEM((lines, depth), f32),
            pltpu.VMEM((rows, depth), f32),
        ],
        compiler_params=pltpu.CompilerParams(vmem_limit_bytes=VMEM_LIMIT),
    )(
        first,
        second,
        third,
        jnp.asarray(depth_high),
        jnp.asarray(depth_low),
        jnp.asarray(left_table(cosine_matrix(lines))),
        jnp.asarray(left_table(cosine_matrix(rows))),
        *box_tables(rows, lines, depth),
    )


def inverse(spectrum, wide_flux, narrow_flux, level):
    lines, rows, depth = spectrum.shape
    steps, groups = rows // BLOCK, lines // GROUP
    depth_high, depth_low = halves(cosine_matrix(depth))
    return pl.pallas_call(
        functools.partial(inverse_kernel, groups),
        grid=(steps + groups,),
        out_shape=jax.ShapeDtypeStruct((rows, lines, depth), jnp.float32),
        in_specs=[
            pl.BlockSpec((GROUP, rows, depth), lambda s: (jnp.minimum(s, groups - 1), 0, 0)),
            pl.BlockSpec((2, GROUP, depth), lambda s: (0, jnp.minimum(s, groups - 1), 0)),
            whole(2, rows, depth),
            whole(1, depth),
        ]
        + table_specs(rows, lines, depth),
        out_specs=pl.BlockSpec((BLOCK, lines, depth), lambda s: (jnp.maximum(s - groups, 0), 0, 0)),
        scratch_shapes=[pltpu.VMEM((depth // LANES, rows * lines, LANES), jnp.float32)],
        compiler_params=pltpu.CompilerParams(vmem_limit_bytes=VMEM_LIMIT),
    )(
        spectrum,
        wide_flux,
        narrow_flux,
        level,
        jnp.asarray(depth_high),
        jnp.asarray(depth_low),
        jnp.asarray(left_table(cosine_matrix(lines).T)),
        jnp.asarray(left_table(cosine_matrix(rows).T)),
        *box_tables(rows, lines, depth),
    )


def own(table, place, count):
    return lax.dynamic_slice_in_dim(jnp.asarray(table), place * count, count, axis=0)


def alternate(length):
    return jnp.asarray(signs(length), jnp.float32)


def eigen(index, count):
    half_sine = jnp.sin(index.astype(jnp.float32) * (math.pi / (2 * count)))
    return 4.0 * half_sine * half_sine


def interfaces(traces, t, place, rows, lines, depth, wide, narrow):
    count = traces.shape[1]
    traces = traces.reshape(wide, narrow, count, -1)
    traces = jnp.transpose(traces, (2, 0, 1, 3))
    cut = [lines, 2 * lines, 2 * lines + rows]
    wide_low, wide_high, narrow_low, narrow_high = jnp.split(traces, cut, axis=-1)
    jump_wide = wide_low[:, 1:] - wide_high[:, :-1]
    jump_narrow = narrow_low[:, :, 1:] - narrow_high[:, :, :-1]
    depth_place = place * count + jnp.arange(count)
    steady = depth_place == 0
    depth_part = eigen(depth_place, depth)
    row_zero = jnp.arange(rows) == 0
    line_zero = jnp.arange(lines) == 0
    last = jnp.einsum("mjl,rmk->rjlk", t["narrow_sines"], own(t["narrow_gain"], place, count), precision=HIGHEST)
    first = jnp.where(
        steady[:, None, None, None] & row_zero, jnp.asarray(t["narrow_steady"])[None, :, :, None], last
    )
    eig = (
        depth_part[:, None, None]
        + jnp.asarray(modes(rows), jnp.float32)[:, None]
        + jnp.asarray(modes(lines), jnp.float32)[None, :]
    )
    faces = jnp.asarray(face(rows)[:, None] * face(lines)[None, :], jnp.float32)
    steady_row = steady[:, None, None] & row_zero[:, None]
    zero_mode = steady_row & line_zero
    weight = faces / jnp.where(zero_mode, 1.0, eig)
    weight_first = jnp.where(steady_row & ~line_zero, 0.0, weight)
    weight_last = jnp.swapaxes(jnp.where(zero_mode, 0.0, weight), 1, 2)
    to_wide = jnp.stack([weight_first, weight_first * alternate(rows)[:, None]], axis=2)
    to_narrow = jnp.stack([weight_last, weight_last * alternate(lines)[:, None]], axis=2)
    shift = depth_part[:, None] + jnp.asarray(modes(lines * narrow), jnp.float32)[None, :]
    decay = own(t["wide_decay"], place, count)
    top = -jnp.sqrt(shift / (4.0 + shift)) * decay * (2.0 + decay)
    top = top[:, None, :]
    decay = decay[:, None, :]
    bottom = decay * decay + 2.0 * (1.0 + decay) * jnp.asarray(t["wide_angle"])[None, :, None]
    wide_gain = top / bottom
    flux = jnp.sum(first[:, None] * jump_narrow[:, :, None], axis=3)
    moved = jnp.einsum("rIjk,rksb->rsIjb", flux, to_wide, precision=HIGHEST)
    edge = [(0, 0)] * 3
    moved = jnp.pad(moved, edge + [(0, 1), (0, 0)]) * alternate(lines) - jnp.pad(moved, edge + [(1, 0), (0, 0)])
    jump_wide = jump_wide + moved[:, 0, 1:] - moved[:, 1, :-1]
    jump_wide = jump_wide.reshape(count, wide - 1, narrow * lines)
    joined = jnp.einsum("riy,qy->riq", jump_wide, t["join"], precision=HIGHEST)
    shaped = jnp.einsum("mi,riq->rmq", t["wide_sine"], joined, precision=HIGHEST)
    shaped = shaped * wide_gain
    shaped = jnp.einsum("mi,rmq->riq", t["wide_sine"], shaped, precision=HIGHEST)
    flux_wide = jnp.einsum("riq,qy->riy", shaped, t["join"], precision=HIGHEST)
    flux_wide = flux_wide.reshape(count, wide - 1, narrow, lines)
    flux_wide = jnp.pad(flux_wide, [(0, 0), (1, 1), (0, 0), (0, 0)])
    moved = jnp.einsum("riJb,rbsk->rsiJk", flux_wide, to_narrow, precision=HIGHEST)
    moved = moved[:, :, 1:] * alternate(rows) - moved[:, :, :-1]
    jump_narrow = jump_narrow + moved[:, 0, :, 1:] - moved[:, 1, :, :-1]
    flux_narrow = jnp.sum(last[:, None] * jump_narrow[:, :, None], axis=3)
    mean_flux = flux_wide[0, 1:, :, 0] - flux_wide[0, :-1, :, 0]
    balanced = jnp.einsum("IJ,Jj->Ij", mean_flux, t["balance"], precision=HIGHEST)
    level = jnp.einsum("Ij,jJ->IJ", balanced, t["level_of_flux"], precision=HIGHEST)
    level = level + jnp.einsum("Ij,jJ->IJ", jump_narrow[0, :, :, 0], t["level_of_jump"], precision=HIGHEST)
    level = level + jnp.einsum("Ii,i->I", t["wide_levels"], joined[0, :, 0], precision=HIGHEST)[:, None]
    flux_narrow = jnp.where(
        steady[:, None, None, None] & row_zero, balanced[None, :, :, None], flux_narrow
    )
    flux_narrow = jnp.pad(flux_narrow, [(0, 0), (0, 0), (1, 1), (0, 0)])
    level = jnp.broadcast_to(level[None, :, :, None], (count, wide, narrow, 8))
    out = jnp.concatenate(
        [flux_wide[:, :-1], flux_wide[:, 1:], flux_narrow[:, :, :-1], flux_narrow[:, :, 1:], level], axis=-1
    )
    out = jnp.transpose(out, (1, 2, 0, 3))
    return out.reshape(wide * narrow, count, -1)


def shards(slope_first, slope_second, slope_third):
    rows, lines, depth = slope_first.shape
    wide = lax.axis_size("wide")
    narrow = lax.axis_size("narrow")
    wide_place = lax.axis_index("wide")
    narrow_place = lax.axis_index("narrow")
    place = wide_place * narrow + narrow_place
    devices = wide * narrow
    t = tables(rows, lines, depth, wide, narrow)
    spectrum, wide_traces, narrow_traces = forward(slope_first, slope_second, slope_third)
    traces = jnp.concatenate([wide_traces.reshape(2 * lines, depth), narrow_traces.reshape(2 * rows, depth)], axis=0)
    traces = jnp.transpose(traces).reshape(devices, depth // devices, -1)
    traces = lax.all_to_all(traces, ("wide", "narrow"), split_axis=0, concat_axis=0, tiled=True)
    fluxes = interfaces(traces, t, place, rows, lines, depth, wide, narrow)
    fluxes = lax.all_to_all(fluxes, ("wide", "narrow"), split_axis=0, concat_axis=0, tiled=True)
    fluxes = jnp.transpose(fluxes.reshape(depth, -1))
    wide_flux = fluxes[: 2 * lines].reshape(2, lines, depth)
    narrow_flux = fluxes[2 * lines : 2 * (lines + rows)].reshape(2, rows, depth)
    level = fluxes[2 * (lines + rows) :][:1]
    return inverse(spectrum, wide_flux, narrow_flux, level)


def solution(mesh):
    placed = P("wide", "narrow", None)
    return jax.shard_map(shards, mesh=mesh, in_specs=(placed, placed, placed), out_specs=placed, check_vma=False)
```

```python
import functools
import math

import jax
import jax.numpy as jnp
import numpy as np
from jax import lax
from jax.experimental import pallas as pl
from jax.experimental.pallas import tpu as pltpu
from jax.sharding import PartitionSpec as P

HIGHEST = lax.Precision.HIGHEST


LANES = 128


def cosine_matrix(length):
    k = np.arange(length)[:, None]
    n = np.arange(length)[None, :]
    table = np.sqrt(2.0 / length) * np.cos(np.pi * ((2 * n + 1) * k % (4 * length)) / (2 * length))
    table[0] = np.sqrt(1.0 / length)
    return table


def sine_matrix(parts):
    m = np.arange(1, parts)
    return np.sqrt(2.0 / parts) * np.sin(np.pi * m[:, None] * m[None, :] / parts)


def modes(length):
    return 4.0 * np.sin(np.pi * np.arange(length) / (2 * length)) ** 2


def signs(length):
    return (-1.0) ** np.arange(length)


def face(length):
    return cosine_matrix(length)[:, 0]


def exponent(mu):
    return 2.0 * np.arcsinh(np.sqrt(mu) / 2.0)


def interface_gain(mu, cells, parts):
    kappa = exponent(mu)[..., None]
    angle = np.pi * np.arange(1, parts) / parts
    decay = np.exp(-kappa * cells)
    ratio = -np.expm1(-2.0 * kappa * cells) / (np.expm1(-kappa * cells) ** 2 + 2.0 * decay * (1.0 - np.cos(angle)))
    return np.tanh(kappa / 2.0) * ratio


def running_levels(parts):
    part = np.arange(parts)[:, None]
    step = np.arange(1, parts)[None, :]
    return (step <= part) - (parts - step) / parts


@functools.lru_cache(None)
def tables(rows, lines, depth, wide, narrow):
    t = {}
    row_modes, line_modes, depth_modes = modes(rows), modes(lines), modes(depth)
    row_face, line_face = face(rows), face(lines)
    sine_n = sine_matrix(narrow)
    gain = interface_gain(depth_modes[:, None] + row_modes[None, :], lines, narrow)
    gain[0, 0, :] = 0.0
    t["narrow_gain"] = np.swapaxes(gain, 1, 2)
    t["narrow_sines"] = np.einsum("jm,ml->mjl", sine_n, sine_n)
    levels_n = running_levels(narrow)
    t["narrow_steady"] = np.cumsum(-levels_n / line_face[0], axis=0)[:-1] / line_face[0]
    full = cosine_matrix(lines * narrow)
    local = cosine_matrix(lines)
    t["join"] = np.einsum("qJn,kn->qJk", full.reshape(lines * narrow, narrow, lines), local).reshape(
        lines * narrow, lines * narrow
    )
    t["wide_decay"] = np.expm1(-exponent(depth_modes[:, None] + modes(lines * narrow)[None, :]) * rows)
    t["wide_sine"] = sine_matrix(wide)
    t["wide_angle"] = 1.0 - np.cos(np.pi * np.arange(1, wide) / wide)
    t["wide_levels"] = -running_levels(wide) / (row_face[0] * math.sqrt(narrow))
    balance = -(row_face[0] / line_face[0]) * np.tril(np.ones((narrow - 1, narrow)))
    t["balance"] = balance.T
    k = np.arange(1, lines)
    near = np.sum(line_face[k] ** 2 / line_modes[k])
    far = np.sum(signs(lines)[k] * line_face[k] ** 2 / line_modes[k])
    link = (1.0 + 2.0 * near) * np.eye(narrow - 1) - far * (np.eye(narrow - 1, k=1) + np.eye(narrow - 1, k=-1))
    t["level_of_flux"] = (levels_n @ link / line_face[0]).T
    t["level_of_jump"] = (-levels_n / line_face[0]).T
    return {name: np.ascontiguousarray(value, dtype=np.float32) for name, value in t.items()}


def halves(table):
    table = np.asarray(table, np.float32)
    high = table.astype(jnp.bfloat16)
    low = (table - high.astype(np.float32)).astype(jnp.bfloat16)
    return high, low


def left_table(table):
    high, low = halves(table)
    return np.block([[high, high], [low, np.zeros_like(low)]])


def split(x):
    high = x.astype(jnp.bfloat16)
    return high, (x - high.astype(jnp.float32)).astype(jnp.bfloat16)


def dot(a, b):
    return jnp.dot(a, b, preferred_element_type=jnp.float32)


def from_left(table, x):
    both = dot(table, jnp.concatenate(split(x), axis=0))
    count = x.shape[0]
    return both[:count] + both[count:]


def from_right(x, high_table, low_table):
    high, low = split(x)
    return dot(high, high_table) + dot(low, high_table) + dot(high, low_table)


def lower_neighbour(x, axis):
    index = lax.broadcasted_iota(jnp.int32, x.shape, axis)
    x = jnp.where(index < x.shape[axis] - 1, x, 0.0)
    return pltpu.roll(x, 1, axis) - x


def put(held, where, value):
    for panel in range(held.shape[0]):
        held[panel, where, :] = value[:, panel * LANES : (panel + 1) * LANES]


def take(held, where):
    return jnp.concatenate([held[panel, where, :] for panel in range(held.shape[0])], axis=1)


def forward_kernel(
    steps,
    first_ref,
    second_ref,
    third_ref,
    depth_high_ref,
    depth_low_ref,
    line_ref,
    row_ref,
    shift_ref,
    faces_ref,
    line_shift_ref,
    line_face_ref,
    out_ref,
    wide_ref,
    narrow_ref,
    carry,
    held,
    wide_face,
    narrow_face,
):
    step = pl.program_id(0)
    rows, lines = row_ref.shape[0] // 2, line_ref.shape[0] // 2
    block = first_ref.shape[0]
    group = out_ref.shape[0]

    @pl.when(step == 0)
    def _():
        carry[...] = jnp.zeros_like(carry)

    @pl.when(step < steps)
    def _():
        below = carry[...]
        parts = []
        for i in range(block):
            here = first_ref[i]
            if i == block - 1:
                here = jnp.where(step < steps - 1, here, 0.0)
            part = below - here + lower_neighbour(second_ref[i], 0) + lower_neighbour(third_ref[i], 1)
            below = here
            parts.append(part)
            narrow_face[pl.ds(step * block + i, 1), :] = second_ref[i, lines - 1 : lines, :]
        carry[...] = below
        stacked = from_right(jnp.concatenate(parts, axis=0), depth_high_ref[...], depth_low_ref[...])
        for i in range(block):
            part = from_left(line_ref[...], stacked[i * lines : (i + 1) * lines])
            put(held, pl.ds(pl.multiple_of((step * block + i) * lines, 8), lines), part)

    @pl.when(step == steps)
    def _():
        face = from_right(first_ref[block - 1], depth_high_ref[...], depth_low_ref[...])
        wide_face[...] = from_left(line_ref[...], face)
        face = from_right(narrow_face[...], depth_high_ref[...], depth_low_ref[...])
        narrow_ref[0] = jnp.zeros_like(face)
        narrow_ref[1] = from_left(row_ref[...], face)

    @pl.when(step >= steps)
    def _():
        lows, highs = [], []
        narrow_low, narrow_high = narrow_ref[0], narrow_ref[1]
        for i in range(group):
            line = (step - steps) * group + i
            part = from_left(row_ref[...], take(held, pl.ds(line, rows, stride=lines)))
            out_ref[i] = part
            eig = shift_ref[...] + line_shift_ref[line]
            closed = jnp.where(eig > 0.0, part / eig, 0.0)
            lows.append(jnp.sum(closed * faces_ref[0], axis=0, keepdims=True))
            highs.append(jnp.sum(closed * faces_ref[1], axis=0, keepdims=True))
            closed = closed * line_face_ref[line]
            narrow_low = narrow_low + closed
            narrow_high = narrow_high + closed if i % 2 == 0 else narrow_high - closed
        wide_ref[0] = jnp.concatenate(lows, axis=0)
        here = pl.ds(pl.multiple_of((step - steps) * group, 8), group)
        wide_ref[1] = jnp.concatenate(highs, axis=0) + wide_face[here, :]
        narrow_ref[0] = narrow_low
        narrow_ref[1] = narrow_high


def inverse_kernel(
    steps,
    spectrum_ref,
    wide_ref,
    narrow_ref,
    level_ref,
    depth_high_ref,
    depth_low_ref,
    line_ref,
    row_ref,
    shift_ref,
    faces_ref,
    line_shift_ref,
    line_face_ref,
    out_ref,
    held,
):
    step = pl.program_id(0)
    rows, lines = row_ref.shape[0] // 2, line_ref.shape[0] // 2
    block = out_ref.shape[0]
    group = spectrum_ref.shape[0]

    @pl.when(step < steps)
    def _():
        for i in range(group):
            line = step * group + i
            added = faces_ref[1] * wide_ref[1, i : i + 1, :] - faces_ref[0] * wide_ref[0, i : i + 1, :]
            turned = narrow_ref[1] if i % 2 == 0 else -narrow_ref[1]
            part = spectrum_ref[i] + added + line_face_ref[line] * (turned - narrow_ref[0])
            eig = shift_ref[...] + line_shift_ref[line]
            part = jnp.where(eig > 0.0, part / eig, level_ref[:1])
            put(held, pl.ds(line, rows, stride=lines), from_left(row_ref[...], part))

    @pl.when(step >= steps)
    def _():
        parts = []
        for i in range(block):
            here = pl.multiple_of(((step - steps) * block + i) * lines, 8)
            parts.append(from_left(line_ref[...], take(held, pl.ds(here, lines))))
        result = from_right(jnp.concatenate(parts, axis=0), depth_high_ref[...], depth_low_ref[...])
        for i in range(block):
            out_ref[i] = result[i * lines : (i + 1) * lines]


MESH = pl.DeviceIdType.MESH


def greet(wide, narrow):
    w, n = lax.axis_index("wide"), lax.axis_index("narrow")
    barrier = pltpu.get_barrier_semaphore()
    for d in range(1, narrow):
        pl.semaphore_signal(barrier, inc=1, device_id=(w, lax.rem(n + d, narrow)), device_id_type=MESH)
    for d in range(1, wide):
        pl.semaphore_signal(barrier, inc=1, device_id=(lax.rem(w + d, wide), n), device_id_type=MESH)
    pl.semaphore_wait(barrier, wide + narrow - 2)


def trade(axis, source, target, send, recv):
    w, n = lax.axis_index("wide"), lax.axis_index("narrow")
    peers = source.shape[0]
    here = w if axis == "wide" else n
    copies = []
    for d in range(1, peers):
        to = lax.rem(here + d, peers)
        copies.append(
            pltpu.make_async_remote_copy(
                src_ref=source.at[to],
                dst_ref=target.at[here],
                send_sem=send.at[d],
                recv_sem=recv.at[d],
                device_id=(to, n) if axis == "wide" else (w, to),
                device_id_type=MESH,
            )
        )
    for copy in copies:
        copy.start()
    target[here] = source[here]
    for copy in copies:
        copy.wait()


def turn(source, target):
    outer = source.shape[0]
    inner = target.shape[0]
    count = source.shape[1] // inner
    for a in range(outer):
        for b in range(inner):
            target[b, a * count : (a + 1) * count, :] = source[a, b * count : (b + 1) * count, :]


def gather_kernel(wide_ref, narrow_ref, out_ref, first, near, turned, near_send, near_recv, far_send, far_recv):
    narrow, far_rows, width = first.shape
    wide = turned.shape[0]
    parts = [wide_ref[0], wide_ref[1], narrow_ref[0], narrow_ref[1]]
    depth = parts[0].shape[1]
    parts.append(jnp.zeros((width - sum(p.shape[0] for p in parts), depth), jnp.float32))
    values = jnp.concatenate(parts, axis=0).T
    for p in range(narrow):
        first[p] = values[p * far_rows : (p + 1) * far_rows]
    greet(wide, narrow)
    trade("narrow", first, near, near_send, near_recv)
    turn(near, turned)
    trade("wide", turned, out_ref, far_send, far_recv)


def scatter_kernel(in_ref, wide_ref, narrow_ref, level_ref, far, turned, near, near_send, near_recv, far_send, far_recv):
    narrow = near.shape[0]
    wide = far.shape[0]
    greet(wide, narrow)
    trade("wide", in_ref, far, far_send, far_recv)
    turn(far, turned)
    trade("narrow", turned, near, near_send, near_recv)
    values = jnp.concatenate([near[p] for p in range(narrow)], axis=0).T
    lines, rows = wide_ref.shape[1], narrow_ref.shape[1]
    wide_ref[0] = values[:lines]
    wide_ref[1] = values[lines : 2 * lines]
    narrow_ref[0] = values[2 * lines : 2 * lines + rows]
    narrow_ref[1] = values[2 * lines + rows : 2 * (lines + rows)]
    level_ref[...] = values[2 * (lines + rows) : 2 * (lines + rows) + 8]


def message_width(rows, lines):
    return -(-(2 * (rows + lines) + 8) // LANES) * LANES


IN_VMEM = pl.BlockSpec(memory_space=pltpu.VMEM)


def semaphores(wide, narrow):
    return [pltpu.SemaphoreType.DMA((k,)) for k in (narrow, narrow, wide, wide)]


def gather(wide_traces, narrow_traces, wide, narrow):
    lines, depth = wide_traces.shape[1:]
    rows = narrow_traces.shape[1]
    count = depth // (wide * narrow)
    width = message_width(rows, lines)
    near = (narrow, wide * count, width)
    far = (wide, narrow * count, width)
    return pl.pallas_call(
        gather_kernel,
        out_shape=jax.ShapeDtypeStruct(far, jnp.float32),
        in_specs=[IN_VMEM, IN_VMEM],
        out_specs=IN_VMEM,
        scratch_shapes=[pltpu.VMEM(v, jnp.float32) for v in (near, near, far)] + semaphores(wide, narrow),
        compiler_params=pltpu.CompilerParams(collective_id=0, has_side_effects=True),
    )(wide_traces, narrow_traces)


def scatter(fluxes, rows, lines, depth):
    wide, _, width = fluxes.shape
    narrow = lax.axis_size("narrow")
    count = depth // (wide * narrow)
    near = (narrow, wide * count, width)
    far = (wide, narrow * count, width)
    f32 = jnp.float32
    return pl.pallas_call(
        scatter_kernel,
        out_shape=[
            jax.ShapeDtypeStruct((2, lines, depth), f32),
            jax.ShapeDtypeStruct((2, rows, depth), f32),
            jax.ShapeDtypeStruct((8, depth), f32),
        ],
        in_specs=[IN_VMEM],
        out_specs=[IN_VMEM] * 3,
        scratch_shapes=[pltpu.VMEM(v, f32) for v in (far, near, near)] + semaphores(wide, narrow),
        compiler_params=pltpu.CompilerParams(collective_id=1, has_side_effects=True),
    )(fluxes)


VMEM_LIMIT = 60 * 2**20
BLOCK = 16
GROUP = 16


def box_tables(rows, lines, depth):
    shift = modes(rows)[:, None] + modes(depth)[None, :]
    low = np.broadcast_to(face(rows)[:, None], (rows, depth))
    high = np.broadcast_to((face(rows) * signs(rows))[:, None], (rows, depth))
    faces = np.stack([low, high])
    return [jnp.asarray(v, jnp.float32) for v in (shift, faces, modes(lines), face(lines))]


def whole(*shape):
    return pl.BlockSpec(shape, lambda s: (0,) * len(shape))


def table_specs(rows, lines, depth):
    return [
        whole(depth, depth),
        whole(depth, depth),
        whole(2 * lines, 2 * lines),
        whole(2 * rows, 2 * rows),
        whole(rows, depth),
        whole(2, rows, depth),
        pl.BlockSpec(memory_space=pltpu.SMEM),
        pl.BlockSpec(memory_space=pltpu.SMEM),
    ]


def forward(first, second, third):
    rows, lines, depth = first.shape
    steps, groups = rows // BLOCK, lines // GROUP
    slab = pl.BlockSpec((BLOCK, lines, depth), lambda s: (jnp.minimum(s, steps - 1), 0, 0))
    depth_high, depth_low = halves(cosine_matrix(depth).T)
    f32 = jnp.float32
    return pl.pallas_call(
        functools.partial(forward_kernel, steps),
        grid=(steps + groups,),
        out_shape=[
            jax.ShapeDtypeStruct((lines, rows, depth), f32),
            jax.ShapeDtypeStruct((2, lines, depth), f32),
            jax.ShapeDtypeStruct((2, rows, depth), f32),
        ],
        in_specs=[slab, slab, slab] + table_specs(rows, lines, depth),
        out_specs=[
            pl.BlockSpec((GROUP, rows, depth), lambda s: (jnp.maximum(s - steps, 0), 0, 0)),
            pl.BlockSpec((2, GROUP, depth), lambda s: (0, jnp.maximum(s - steps, 0), 0)),
            whole(2, rows, depth),
        ],
        scratch_shapes=[
            pltpu.VMEM((lines, depth), f32),
            pltpu.VMEM((depth // LANES, rows * lines, LANES), f32),
            pltpu.VMEM((lines, depth), f32),
            pltpu.VMEM((rows, depth), f32),
        ],
        compiler_params=pltpu.CompilerParams(vmem_limit_bytes=VMEM_LIMIT),
    )(
        first,
        second,
        third,
        jnp.asarray(depth_high),
        jnp.asarray(depth_low),
        jnp.asarray(left_table(cosine_matrix(lines))),
        jnp.asarray(left_table(cosine_matrix(rows))),
        *box_tables(rows, lines, depth),
    )


def inverse(spectrum, wide_flux, narrow_flux, level):
    lines, rows, depth = spectrum.shape
    steps, groups = rows // BLOCK, lines // GROUP
    depth_high, depth_low = halves(cosine_matrix(depth))
    return pl.pallas_call(
        functools.partial(inverse_kernel, groups),
        grid=(steps + groups,),
        out_shape=jax.ShapeDtypeStruct((rows, lines, depth), jnp.float32),
        in_specs=[
            pl.BlockSpec((GROUP, rows, depth), lambda s: (jnp.minimum(s, groups - 1), 0, 0)),
            pl.BlockSpec((2, GROUP, depth), lambda s: (0, jnp.minimum(s, groups - 1), 0)),
            whole(2, rows, depth),
            whole(8, depth),
        ]
        + table_specs(rows, lines, depth),
        out_specs=pl.BlockSpec((BLOCK, lines, depth), lambda s: (jnp.maximum(s - groups, 0), 0, 0)),
        scratch_shapes=[pltpu.VMEM((depth // LANES, rows * lines, LANES), jnp.float32)],
        compiler_params=pltpu.CompilerParams(vmem_limit_bytes=VMEM_LIMIT),
    )(
        spectrum,
        wide_flux,
        narrow_flux,
        level,
        jnp.asarray(depth_high),
        jnp.asarray(depth_low),
        jnp.asarray(left_table(cosine_matrix(lines).T)),
        jnp.asarray(left_table(cosine_matrix(rows).T)),
        *box_tables(rows, lines, depth),
    )


def own(table, place, count):
    return lax.dynamic_slice_in_dim(jnp.asarray(table), place * count, count, axis=0)


def alternate(length):
    return jnp.asarray(signs(length), jnp.float32)


def eigen(index, count):
    half_sine = jnp.sin(index.astype(jnp.float32) * (math.pi / (2 * count)))
    return 4.0 * half_sine * half_sine


def interfaces(traces, t, place, rows, lines, depth, wide, narrow):
    count = traces.shape[1] // narrow
    traces = traces.reshape(wide, narrow, count, -1)
    traces = jnp.transpose(traces, (2, 0, 1, 3))
    cut = [lines, 2 * lines, 2 * lines + rows, 2 * (lines + rows)]
    wide_low, wide_high, narrow_low, narrow_high, _ = jnp.split(traces, cut, axis=-1)
    jump_wide = wide_low[:, 1:] - wide_high[:, :-1]
    jump_narrow = narrow_low[:, :, 1:] - narrow_high[:, :, :-1]
    depth_place = place * count + jnp.arange(count)
    steady = depth_place == 0
    depth_part = eigen(depth_place, depth)
    row_zero = jnp.arange(rows) == 0
    line_zero = jnp.arange(lines) == 0
    last = jnp.einsum("mjl,rmk->rjlk", t["narrow_sines"], own(t["narrow_gain"], place, count), precision=HIGHEST)
    first = jnp.where(
        steady[:, None, None, None] & row_zero, jnp.asarray(t["narrow_steady"])[None, :, :, None], last
    )
    eig = (
        depth_part[:, None, None]
        + jnp.asarray(modes(rows), jnp.float32)[:, None]
        + jnp.asarray(modes(lines), jnp.float32)[None, :]
    )
    faces = jnp.asarray(face(rows)[:, None] * face(lines)[None, :], jnp.float32)
    steady_row = steady[:, None, None] & row_zero[:, None]
    zero_mode = steady_row & line_zero
    weight = faces / jnp.where(zero_mode, 1.0, eig)
    weight_first = jnp.where(steady_row & ~line_zero, 0.0, weight)
    weight_last = jnp.swapaxes(jnp.where(zero_mode, 0.0, weight), 1, 2)
    to_wide = jnp.stack([weight_first, weight_first * alternate(rows)[:, None]], axis=2)
    to_narrow = jnp.stack([weight_last, weight_last * alternate(lines)[:, None]], axis=2)
    shift = depth_part[:, None] + jnp.asarray(modes(lines * narrow), jnp.float32)[None, :]
    decay = own(t["wide_decay"], place, count)
    top = -jnp.sqrt(shift / (4.0 + shift)) * decay * (2.0 + decay)
    top = top[:, None, :]
    decay = decay[:, None, :]
    bottom = decay * decay + 2.0 * (1.0 + decay) * jnp.asarray(t["wide_angle"])[None, :, None]
    wide_gain = top / bottom
    flux = jnp.sum(first[:, None] * jump_narrow[:, :, None], axis=3)
    moved = jnp.einsum("rIjk,rksb->rsIjb", flux, to_wide, precision=HIGHEST)
    edge = [(0, 0)] * 3
    moved = jnp.pad(moved, edge + [(0, 1), (0, 0)]) * alternate(lines) - jnp.pad(moved, edge + [(1, 0), (0, 0)])
    jump_wide = jump_wide + moved[:, 0, 1:] - moved[:, 1, :-1]
    jump_wide = jump_wide.reshape(count, wide - 1, narrow * lines)
    joined = jnp.einsum("riy,qy->riq", jump_wide, t["join"], precision=HIGHEST)
    shaped = jnp.einsum("mi,riq->rmq", t["wide_sine"], joined, precision=HIGHEST)
    shaped = shaped * wide_gain
    shaped = jnp.einsum("mi,rmq->riq", t["wide_sine"], shaped, precision=HIGHEST)
    flux_wide = jnp.einsum("riq,qy->riy", shaped, t["join"], precision=HIGHEST)
    flux_wide = flux_wide.reshape(count, wide - 1, narrow, lines)
    flux_wide = jnp.pad(flux_wide, [(0, 0), (1, 1), (0, 0), (0, 0)])
    moved = jnp.einsum("riJb,rbsk->rsiJk", flux_wide, to_narrow, precision=HIGHEST)
    moved = moved[:, :, 1:] * alternate(rows) - moved[:, :, :-1]
    jump_narrow = jump_narrow + moved[:, 0, :, 1:] - moved[:, 1, :, :-1]
    flux_narrow = jnp.sum(last[:, None] * jump_narrow[:, :, None], axis=3)
    mean_flux = flux_wide[0, 1:, :, 0] - flux_wide[0, :-1, :, 0]
    balanced = jnp.einsum("IJ,Jj->Ij", mean_flux, t["balance"], precision=HIGHEST)
    level = jnp.einsum("Ij,jJ->IJ", balanced, t["level_of_flux"], precision=HIGHEST)
    level = level + jnp.einsum("Ij,jJ->IJ", jump_narrow[0, :, :, 0], t["level_of_jump"], precision=HIGHEST)
    level = level + jnp.einsum("Ii,i->I", t["wide_levels"], joined[0, :, 0], precision=HIGHEST)[:, None]
    flux_narrow = jnp.where(
        steady[:, None, None, None] & row_zero, balanced[None, :, :, None], flux_narrow
    )
    flux_narrow = jnp.pad(flux_narrow, [(0, 0), (0, 0), (1, 1), (0, 0)])
    level = jnp.broadcast_to(level[None, :, :, None], (count, wide, narrow, message_width(rows, lines) - 2 * (rows + lines)))
    out = jnp.concatenate(
        [flux_wide[:, :-1], flux_wide[:, 1:], flux_narrow[:, :, :-1], flux_narrow[:, :, 1:], level], axis=-1
    )
    out = jnp.transpose(out, (1, 2, 0, 3))
    return out.reshape(wide, narrow * count, -1)


def shards(slope_first, slope_second, slope_third):
    rows, lines, depth = slope_first.shape
    wide = lax.axis_size("wide")
    narrow = lax.axis_size("narrow")
    wide_place = lax.axis_index("wide")
    narrow_place = lax.axis_index("narrow")
    place = narrow_place * wide + wide_place
    t = tables(rows, lines, depth, wide, narrow)
    spectrum, wide_traces, narrow_traces = forward(slope_first, slope_second, slope_third)
    traces = gather(wide_traces, narrow_traces, wide, narrow)
    fluxes = interfaces(traces, t, place, rows, lines, depth, wide, narrow)
    wide_flux, narrow_flux, level = scatter(fluxes, rows, lines, depth)
    return inverse(spectrum, wide_flux, narrow_flux, level)


def solution(mesh):
    placed = P("wide", "narrow", None)
    return jax.shard_map(shards, mesh=mesh, in_specs=(placed, placed, placed), out_specs=placed, check_vma=False)
```

```python
import functools
import math

import jax
import jax.numpy as jnp
import numpy as np
from jax import lax
from jax.experimental import pallas as pl
from jax.experimental.pallas import tpu as pltpu
from jax.sharding import PartitionSpec as P

HIGHEST = lax.Precision.HIGHEST


LANES = 128


def cosine_matrix(length):
    k = np.arange(length)[:, None]
    n = np.arange(length)[None, :]
    table = np.sqrt(2.0 / length) * np.cos(np.pi * ((2 * n + 1) * k % (4 * length)) / (2 * length))
    table[0] = np.sqrt(1.0 / length)
    return table


def sine_matrix(parts):
    m = np.arange(1, parts)
    return np.sqrt(2.0 / parts) * np.sin(np.pi * m[:, None] * m[None, :] / parts)


def modes(length):
    return 4.0 * np.sin(np.pi * np.arange(length) / (2 * length)) ** 2


def signs(length):
    return (-1.0) ** np.arange(length)


def face(length):
    return cosine_matrix(length)[:, 0]


def exponent(mu):
    return 2.0 * np.arcsinh(np.sqrt(mu) / 2.0)


def interface_gain(mu, cells, parts):
    kappa = exponent(mu)[..., None]
    angle = np.pi * np.arange(1, parts) / parts
    decay = np.exp(-kappa * cells)
    ratio = -np.expm1(-2.0 * kappa * cells) / (np.expm1(-kappa * cells) ** 2 + 2.0 * decay * (1.0 - np.cos(angle)))
    return np.tanh(kappa / 2.0) * ratio


def running_levels(parts):
    part = np.arange(parts)[:, None]
    step = np.arange(1, parts)[None, :]
    return (step <= part) - (parts - step) / parts


def bordered(matrix, top, left):
    return np.pad(matrix, ((top, 0), (left, 0)))


def lane_padded(table):
    pad = [(0, 0)] * (table.ndim - 1) + [(0, -table.shape[-1] % LANES)]
    return np.pad(table, pad)


@functools.lru_cache(None)
def tables(rows, lines, depth, wide, narrow):
    count = depth // (wide * narrow)
    row_modes, line_modes, depth_modes = modes(rows), modes(lines), modes(depth)
    row_face, line_face = face(rows), face(lines)
    own_all = np.eye(count)
    own_first = np.zeros((count, count))
    own_first[0, 0] = 1.0

    def over_narrow(matrix, own):
        return np.kron(np.eye(wide), np.kron(matrix, own))

    t = {}
    t["sine"] = over_narrow(bordered(sine_matrix(narrow), 1, 1), own_all)
    levels = running_levels(narrow)
    steady = np.cumsum(-levels / line_face[0], axis=0)[:-1] / line_face[0]
    t["steady"] = over_narrow(bordered(steady, 1, 1), own_first)
    balance = -(row_face[0] / line_face[0]) * np.tril(np.ones((narrow - 1, narrow)))
    t["balance"] = over_narrow(bordered(balance, 1, 0), own_first)
    k = np.arange(1, lines)
    near = np.sum(line_face[k] ** 2 / line_modes[k])
    far = np.sum(signs(lines)[k] * line_face[k] ** 2 / line_modes[k])
    link = (1.0 + 2.0 * near) * np.eye(narrow - 1) - far * (np.eye(narrow - 1, k=1) + np.eye(narrow - 1, k=-1))
    t["level_flux"] = over_narrow(bordered(levels @ link / line_face[0], 0, 1), own_first)
    t["level_jump"] = over_narrow(bordered(-levels / line_face[0], 0, 1), own_first)
    level_wide = bordered(-running_levels(wide) / (row_face[0] * math.sqrt(narrow)), 0, 1)
    first_column = np.zeros((count, 1))
    first_column[0, 0] = 1.0
    t["level_wide"] = np.kron(first_column.T, np.kron(level_wide, np.kron(np.ones((narrow, 1)), first_column)))
    gain = interface_gain(depth_modes[:, None] + row_modes[None, :], lines, narrow)
    gain[0, 0, :] = 0.0
    gain = bordered(np.moveaxis(gain, 2, 1).reshape(depth * (narrow - 1), rows), 0, 0)
    gain = np.pad(gain.reshape(depth, narrow - 1, rows), ((0, 0), (1, 0), (0, 0)))
    gain = gain.reshape(wide * narrow, count, narrow, rows).swapaxes(1, 2)
    t["gain"] = lane_padded(gain.reshape(wide * narrow, narrow * count, rows))
    full = cosine_matrix(lines * narrow).reshape(lines * narrow, narrow, lines)
    t["join"] = np.einsum("qJn,kn->Jkq", full, cosine_matrix(lines))
    shift = depth_modes[:, None] + modes(lines * narrow)[None, :]
    decay = np.expm1(-exponent(shift) * rows)
    top = -np.sqrt(shift / (4.0 + shift)) * decay * (2.0 + decay)
    t["decay"] = np.stack([decay, top], axis=1).reshape(-1, 8, lines * narrow)
    t["wide_sine"] = np.kron(own_all, bordered(sine_matrix(wide), 1, 1))
    angle = 1.0 - np.cos(np.pi * np.arange(wide) / wide)
    angle[0] = 1.0
    t["angle"] = np.broadcast_to(angle[:, None], (wide, lines * narrow))
    t["box_modes"] = row_modes[:, None] + line_modes[None, :]
    both = row_face[:, None] * line_face[None, :]
    t["faces"] = np.stack([both, both * signs(rows)[:, None]])
    t["box_modes_turned"] = t["box_modes"].T
    t["faces_turned"] = np.stack([both.T, both.T * signs(lines)[:, None]])
    t["alternate"] = np.broadcast_to(signs(LANES)[None, :], (8, LANES))
    return {name: np.ascontiguousarray(value, dtype=np.float32) for name, value in t.items()}


FIXED = (
    "sine",
    "steady",
    "balance",
    "level_flux",
    "level_jump",
    "level_wide",
    "join",
    "wide_sine",
    "angle",
    "box_modes",
    "faces",
    "box_modes_turned",
    "faces_turned",
    "alternate",
)


def halves(table):
    table = np.asarray(table, np.float32)
    high = table.astype(jnp.bfloat16)
    low = (table - high.astype(np.float32)).astype(jnp.bfloat16)
    return high, low


def left_table(table):
    high, low = halves(table)
    return np.block([[high, high], [low, np.zeros_like(low)]])


def split(x):
    high = x.astype(jnp.bfloat16)
    return high, (x - high.astype(jnp.float32)).astype(jnp.bfloat16)


def dot(a, b):
    return jnp.dot(a, b, preferred_element_type=jnp.float32)


def from_left(table, x):
    both = dot(table, jnp.concatenate(split(x), axis=0))
    count = x.shape[0]
    return both[:count] + both[count:]


def from_right(x, high_table, low_table):
    high, low = split(x)
    return dot(high, high_table) + dot(low, high_table) + dot(high, low_table)


def lower_neighbour(x, axis):
    index = lax.broadcasted_iota(jnp.int32, x.shape, axis)
    x = jnp.where(index < x.shape[axis] - 1, x, 0.0)
    return pltpu.roll(x, 1, axis) - x


def put(held, where, value):
    for panel in range(held.shape[0]):
        held[panel, where, :] = value[:, panel * LANES : (panel + 1) * LANES]


def take(held, where):
    return jnp.concatenate([held[panel, where, :] for panel in range(held.shape[0])], axis=1)


def forward_kernel(
    steps,
    first_ref,
    second_ref,
    third_ref,
    depth_high_ref,
    depth_low_ref,
    line_ref,
    row_ref,
    shift_ref,
    faces_ref,
    line_shift_ref,
    line_face_ref,
    out_ref,
    wide_ref,
    narrow_ref,
    carry,
    held,
    wide_face,
    narrow_face,
):
    step = pl.program_id(0)
    rows, lines = row_ref.shape[0] // 2, line_ref.shape[0] // 2
    block = first_ref.shape[0]
    group = out_ref.shape[0]

    @pl.when(step == 0)
    def _():
        carry[...] = jnp.zeros_like(carry)

    @pl.when(step < steps)
    def _():
        below = carry[...]
        parts = []
        for i in range(block):
            here = first_ref[i]
            if i == block - 1:
                here = jnp.where(step < steps - 1, here, 0.0)
            part = below - here + lower_neighbour(second_ref[i], 0) + lower_neighbour(third_ref[i], 1)
            below = here
            parts.append(part)
            narrow_face[pl.ds(step * block + i, 1), :] = second_ref[i, lines - 1 : lines, :]
        carry[...] = below
        stacked = from_right(jnp.concatenate(parts, axis=0), depth_high_ref[...], depth_low_ref[...])
        for i in range(block):
            part = from_left(line_ref[...], stacked[i * lines : (i + 1) * lines])
            put(held, pl.ds(pl.multiple_of((step * block + i) * lines, 8), lines), part)

    @pl.when(step == steps)
    def _():
        face = from_right(first_ref[block - 1], depth_high_ref[...], depth_low_ref[...])
        wide_face[...] = from_left(line_ref[...], face)
        face = from_right(narrow_face[...], depth_high_ref[...], depth_low_ref[...])
        narrow_ref[0] = jnp.zeros_like(face)
        narrow_ref[1] = from_left(row_ref[...], face)

    @pl.when(step >= steps)
    def _():
        lows, highs = [], []
        narrow_low, narrow_high = narrow_ref[0], narrow_ref[1]
        for i in range(group):
            line = (step - steps) * group + i
            part = from_left(row_ref[...], take(held, pl.ds(line, rows, stride=lines)))
            out_ref[i] = part
            eig = shift_ref[...] + line_shift_ref[line]
            closed = jnp.where(eig > 0.0, part / eig, 0.0)
            lows.append(jnp.sum(closed * faces_ref[0], axis=0, keepdims=True))
            highs.append(jnp.sum(closed * faces_ref[1], axis=0, keepdims=True))
            closed = closed * line_face_ref[line]
            narrow_low = narrow_low + closed
            narrow_high = narrow_high + closed if i % 2 == 0 else narrow_high - closed
        wide_ref[0] = jnp.concatenate(lows, axis=0)
        here = pl.ds(pl.multiple_of((step - steps) * group, 8), group)
        wide_ref[1] = jnp.concatenate(highs, axis=0) + wide_face[here, :]
        narrow_ref[0] = narrow_low
        narrow_ref[1] = narrow_high


def inverse_kernel(
    steps,
    spectrum_ref,
    wide_ref,
    narrow_ref,
    level_ref,
    depth_high_ref,
    depth_low_ref,
    line_ref,
    row_ref,
    shift_ref,
    faces_ref,
    line_shift_ref,
    line_face_ref,
    out_ref,
    held,
):
    step = pl.program_id(0)
    rows, lines = row_ref.shape[0] // 2, line_ref.shape[0] // 2
    block = out_ref.shape[0]
    group = spectrum_ref.shape[0]

    @pl.when(step < steps)
    def _():
        for i in range(group):
            line = step * group + i
            added = faces_ref[1] * wide_ref[1, i : i + 1, :] - faces_ref[0] * wide_ref[0, i : i + 1, :]
            turned = narrow_ref[1] if i % 2 == 0 else -narrow_ref[1]
            part = spectrum_ref[i] + added + line_face_ref[line] * (turned - narrow_ref[0])
            eig = shift_ref[...] + line_shift_ref[line]
            part = jnp.where(eig > 0.0, part / eig, level_ref[:1])
            put(held, pl.ds(line, rows, stride=lines), from_left(row_ref[...], part))

    @pl.when(step >= steps)
    def _():
        parts = []
        for i in range(block):
            here = pl.multiple_of(((step - steps) * block + i) * lines, 8)
            parts.append(from_left(line_ref[...], take(held, pl.ds(here, lines))))
        result = from_right(jnp.concatenate(parts, axis=0), depth_high_ref[...], depth_low_ref[...])
        for i in range(block):
            out_ref[i] = result[i * lines : (i + 1) * lines]


MESH = pl.DeviceIdType.MESH


def greet(wide, narrow):
    w, n = lax.axis_index("wide"), lax.axis_index("narrow")
    barrier = pltpu.get_barrier_semaphore()
    for d in range(1, narrow):
        pl.semaphore_signal(barrier, inc=1, device_id=(w, lax.rem(n + d, narrow)), device_id_type=MESH)
    for d in range(1, wide):
        pl.semaphore_signal(barrier, inc=1, device_id=(lax.rem(w + d, wide), n), device_id_type=MESH)
    pl.semaphore_wait(barrier, wide + narrow - 2)


def trade(axis, source, target, send, recv):
    w, n = lax.axis_index("wide"), lax.axis_index("narrow")
    peers = source.shape[0]
    here = w if axis == "wide" else n
    copies = []
    for d in range(1, peers):
        to = lax.rem(here + d, peers)
        copies.append(
            pltpu.make_async_remote_copy(
                src_ref=source.at[to],
                dst_ref=target.at[here],
                send_sem=send.at[d],
                recv_sem=recv.at[d],
                device_id=(to, n) if axis == "wide" else (w, to),
                device_id_type=MESH,
            )
        )
    for copy in copies:
        copy.start()
    target[here] = source[here]
    for copy in copies:
        copy.wait()


def turn(source, target):
    outer = source.shape[0]
    inner = target.shape[0]
    count = source.shape[1] // inner
    for a in range(outer):
        for b in range(inner):
            target[b, a * count : (a + 1) * count, :] = source[a, b * count : (b + 1) * count, :]


def exact(a, b):
    return jnp.dot(a, b, precision=HIGHEST, preferred_element_type=jnp.float32)


def exact_turned(a, b):
    return lax.dot_general(
        a, b, (((1,), (1,)), ((), ())), precision=HIGHEST, preferred_element_type=jnp.float32
    )


def interfaces(traces, t, gain, decay, modes_ref, place, jumps, fluxes, wide, narrow):
    total = traces.shape[0]
    count = total // (wide * narrow)
    span = narrow * count
    rows, lines = t["box_modes"].shape
    row = lax.broadcasted_iota(jnp.int32, (total, 1), 0)
    has_wide = row >= span
    has_narrow = (row & (span - 1)) >= count
    own_mode = row & (count - 1)
    holds_steady = place == 0

    def up(x, by):
        return pltpu.roll(x, total - by, 0)

    def by_mode(x, weights):
        out = exact(x, weights[0])
        for mode in range(1, count):
            out = jnp.where(own_mode == mode, exact(x, weights[mode]), out)
        return out

    def influence(box_modes, faces, side, first):
        weights = []
        low = lax.broadcasted_iota(jnp.int32, box_modes.shape, 0) == 0
        left = lax.broadcasted_iota(jnp.int32, box_modes.shape, 1) == 0
        for mode in range(count):
            shift = modes_ref[place * count + mode]
            eig = box_modes[...] + shift
            some = eig > 0.0
            value = jnp.where(some, faces[side] / eig, faces[side] if first else 0.0)
            if first and mode == 0:
                value = jnp.where(low & jnp.logical_not(left) & holds_steady, 0.0, value)
            weights.append(value)
        return weights

    alternate = t["alternate"][:1, :]
    wide_low, wide_high = traces[:, :lines], traces[:, LANES : LANES + lines]
    narrow_low, narrow_high = traces[:, 2 * LANES : 2 * LANES + rows], traces[:, 2 * LANES + rows : 2 * LANES + 2 * rows]
    jump_narrow = jnp.where(has_narrow, narrow_low - pltpu.roll(narrow_high, count, 0), 0.0)
    jump_wide = jnp.where(has_wide, wide_low - pltpu.roll(wide_high, span, 0), 0.0)
    gain = jnp.concatenate([gain[:, :rows]] * wide, axis=0)
    sine = t["sine"][...]

    def glued(jump):
        return exact(sine, gain * exact(sine, jump))

    row_zero = lax.broadcasted_iota(jnp.int32, (total, rows), 1) == 0
    flux = glued(jump_narrow)
    steady = exact(t["steady"][...], jump_narrow)
    flux = flux + jnp.where(row_zero & holds_steady, steady, 0.0)
    moved = []
    for side in range(2):
        value = by_mode(flux, influence(t["box_modes"], t["faces"], side, True))
        moved.append(alternate[:, :lines] * up(value, count) - value)
    jump_wide = jump_wide + jnp.where(has_wide, moved[0] - pltpu.roll(moved[1], span, 0), 0.0)
    pad = jnp.zeros((total, LANES - lines), jnp.float32)
    jumps[...] = jnp.concatenate([jump_wide, pad], axis=1)
    joined = jnp.zeros((count * wide, lines * narrow), jnp.float32)
    for J in range(narrow):
        part = [jumps[pl.ds(J * count + mode, wide, stride=span), :] for mode in range(count)]
        joined = joined + exact(jnp.concatenate(part, axis=0)[:, :lines], t["join"][J])
    wide_gain = []
    for mode in range(count):
        at, top = decay[2 * mode : 2 * mode + 1], decay[2 * mode + 1 : 2 * mode + 2]
        wide_gain.append(top / (at * at + 2.0 * (1.0 + at) * t["angle"][...]))
    wide_sine = t["wide_sine"][...]
    shaped = exact(wide_sine, jnp.concatenate(wide_gain, axis=0) * exact(wide_sine, joined))
    pad = jnp.zeros((wide, LANES - lines), jnp.float32)
    for J in range(narrow):
        part = exact_turned(shaped, t["join"][J])
        for mode in range(count):
            fluxes[pl.ds(J * count + mode, wide, stride=span), :] = jnp.concatenate(
                [part[mode * wide : (mode + 1) * wide], pad], axis=1
            )
    padded_wide = fluxes[...]
    flux_wide = padded_wide[:, :lines]
    moved = []
    for side in range(2):
        value = by_mode(flux_wide, influence(t["box_modes_turned"], t["faces_turned"], side, False))
        moved.append(alternate[:, :rows] * up(value, span) - value)
    jump_narrow = jump_narrow + jnp.where(has_narrow, moved[0] - pltpu.roll(moved[1], count, 0), 0.0)
    flux_narrow = glued(jump_narrow)
    padded_high = up(padded_wide, span)
    balanced = exact(t["balance"][...], (padded_high - padded_wide)[:, :rows])
    level = exact(t["level_flux"][...], balanced) + exact(t["level_jump"][...], jump_narrow)
    level = level + exact(t["level_wide"][...], joined[:, :rows])
    flux_narrow = jnp.where(row_zero & (own_mode == 0) & holds_steady, balanced, flux_narrow)
    rest = level[:, : LANES - 2 * rows]
    return jnp.concatenate([padded_wide, padded_high, flux_narrow, up(flux_narrow, count), rest], axis=1)


def exchange_kernel(wide_place_order, *refs):
    wide, narrow = wide_place_order
    names = len(FIXED)
    wide_in, narrow_in = refs[:2]
    sources = refs[2 : 2 + names]
    gain_hbm, decay_hbm, modes_ref, wide_ref, narrow_ref, level_ref = refs[2 + names : 8 + names]
    fixed = refs[8 + names : 8 + 2 * names]
    gain, decay, near_a, near_b, far_a, far_b, near_c, far_c, jumps, fluxes = refs[8 + 2 * names : 18 + 2 * names]
    table_sem, near_send, near_recv, far_send, far_recv, near_send2, near_recv2, far_send2, far_recv2 = refs[18 + 2 * names :]
    lines, depth = wide_in.shape[1:]
    rows = narrow_in.shape[1]
    count = depth // (wide * narrow)
    place = lax.axis_index("narrow") * wide + lax.axis_index("wide")
    per_block = 8 // (2 * count)
    own = [(gain_hbm.at[place], gain), (decay_hbm.at[lax.div(place, per_block)], decay)]
    copies = start_all(list(zip(sources, fixed)) + own, table_sem)
    gap = jnp.zeros((LANES - lines, depth), jnp.float32)
    rest = jnp.zeros((LANES - 2 * rows, depth), jnp.float32)
    values = jnp.concatenate([wide_in[0], gap, wide_in[1], gap, narrow_in[0], narrow_in[1], rest], axis=0).T
    far_rows = wide * count
    for p in range(narrow):
        near_a[p] = values[p * far_rows : (p + 1) * far_rows]
    greet(wide, narrow)
    trade("narrow", near_a, near_b, near_send, near_recv)
    turn(near_b, far_a)
    trade("wide", far_a, far_b, far_send, far_recv)
    for copy in copies:
        copy.wait()
    traces = jnp.concatenate([far_b[p] for p in range(wide)], axis=0)
    here = lax.rem(place, per_block)
    own_decay = decay[: 2 * count]
    for p in range(1, per_block):
        own_decay = jnp.where(here == p, decay[p * 2 * count : (p + 1) * 2 * count], own_decay)
    table = dict(zip(FIXED, fixed))
    out = interfaces(traces, table, gain[...], own_decay, modes_ref, place, jumps, fluxes, wide, narrow)
    span = narrow * count
    for p in range(wide):
        far_a[p] = out[p * span : (p + 1) * span]
    trade("wide", far_a, far_c, far_send2, far_recv2)
    turn(far_c, near_a)
    trade("narrow", near_a, near_c, near_send2, near_recv2)
    values = jnp.concatenate([near_c[p] for p in range(narrow)], axis=0).T
    wide_ref[0] = values[:lines]
    wide_ref[1] = values[LANES : LANES + lines]
    narrow_ref[0] = values[2 * LANES : 2 * LANES + rows]
    narrow_ref[1] = values[2 * LANES + rows : 2 * LANES + 2 * rows]
    level_ref[...] = values[2 * (LANES + rows) : 2 * (LANES + rows) + 8]


def start_all(pairs, sem):
    copies = [pltpu.make_async_copy(source, target, sem.at[i]) for i, (source, target) in enumerate(pairs)]
    for copy in copies:
        copy.start()
    return copies


IN_VMEM = pl.BlockSpec(memory_space=pltpu.VMEM)
IN_HBM = pl.BlockSpec(memory_space=pl.ANY)
IN_SMEM = pl.BlockSpec(memory_space=pltpu.SMEM)


def exchange(wide_traces, narrow_traces, wide, narrow):
    lines, depth = wide_traces.shape[1:]
    rows = narrow_traces.shape[1]
    count = depth // (wide * narrow)
    width = 3 * LANES
    t = tables(rows, lines, depth, wide, narrow)
    near = (narrow, wide * count, width)
    far = (wide, narrow * count, width)
    face_rows = (wide * narrow * count, LANES)
    f32 = jnp.float32
    fixed = [jnp.asarray(t[name]) for name in FIXED]
    shapes = [v.shape for v in fixed] + [t["gain"].shape[1:], t["decay"].shape[1:]]
    shapes += [near, near, far, far, near, far, face_rows, face_rows]
    sems = [len(fixed) + 2, narrow, narrow, wide, wide, narrow, narrow, wide, wide]
    return pl.pallas_call(
        functools.partial(exchange_kernel, (wide, narrow)),
        out_shape=[
            jax.ShapeDtypeStruct((2, lines, depth), f32),
            jax.ShapeDtypeStruct((2, rows, depth), f32),
            jax.ShapeDtypeStruct((8, depth), f32),
        ],
        in_specs=[IN_VMEM, IN_VMEM] + [IN_HBM] * (len(fixed) + 2) + [IN_SMEM],
        out_specs=[IN_VMEM] * 3,
        scratch_shapes=[pltpu.VMEM(v, f32) for v in shapes] + [pltpu.SemaphoreType.DMA((k,)) for k in sems],
        compiler_params=pltpu.CompilerParams(
            collective_id=0, has_side_effects=True, vmem_limit_bytes=VMEM_LIMIT
        ),
    )(
        wide_traces,
        narrow_traces,
        *fixed,
        jnp.asarray(t["gain"]),
        jnp.asarray(t["decay"]),
        jnp.asarray(modes(depth), f32),
    )


VMEM_LIMIT = 60 * 2**20
BLOCK = 16
GROUP = 16


def box_tables(rows, lines, depth):
    shift = modes(rows)[:, None] + modes(depth)[None, :]
    low = np.broadcast_to(face(rows)[:, None], (rows, depth))
    high = np.broadcast_to((face(rows) * signs(rows))[:, None], (rows, depth))
    faces = np.stack([low, high])
    return [jnp.asarray(v, jnp.float32) for v in (shift, faces, modes(lines), face(lines))]


def whole(*shape):
    return pl.BlockSpec(shape, lambda s: (0,) * len(shape))


def table_specs(rows, lines, depth):
    return [
        whole(depth, depth),
        whole(depth, depth),
        whole(2 * lines, 2 * lines),
        whole(2 * rows, 2 * rows),
        whole(rows, depth),
        whole(2, rows, depth),
        pl.BlockSpec(memory_space=pltpu.SMEM),
        pl.BlockSpec(memory_space=pltpu.SMEM),
    ]


def forward(first, second, third):
    rows, lines, depth = first.shape
    steps, groups = rows // BLOCK, lines // GROUP
    slab = pl.BlockSpec((BLOCK, lines, depth), lambda s: (jnp.minimum(s, steps - 1), 0, 0))
    depth_high, depth_low = halves(cosine_matrix(depth).T)
    f32 = jnp.float32
    return pl.pallas_call(
        functools.partial(forward_kernel, steps),
        grid=(steps + groups,),
        out_shape=[
            jax.ShapeDtypeStruct((lines, rows, depth), f32),
            jax.ShapeDtypeStruct((2, lines, depth), f32),
            jax.ShapeDtypeStruct((2, rows, depth), f32),
        ],
        in_specs=[slab, slab, slab] + table_specs(rows, lines, depth),
        out_specs=[
            pl.BlockSpec((GROUP, rows, depth), lambda s: (jnp.maximum(s - steps, 0), 0, 0)),
            pl.BlockSpec((2, GROUP, depth), lambda s: (0, jnp.maximum(s - steps, 0), 0)),
            whole(2, rows, depth),
        ],
        scratch_shapes=[
            pltpu.VMEM((lines, depth), f32),
            pltpu.VMEM((depth // LANES, rows * lines, LANES), f32),
            pltpu.VMEM((lines, depth), f32),
            pltpu.VMEM((rows, depth), f32),
        ],
        compiler_params=pltpu.CompilerParams(vmem_limit_bytes=VMEM_LIMIT),
    )(
        first,
        second,
        third,
        jnp.asarray(depth_high),
        jnp.asarray(depth_low),
        jnp.asarray(left_table(cosine_matrix(lines))),
        jnp.asarray(left_table(cosine_matrix(rows))),
        *box_tables(rows, lines, depth),
    )


def inverse(spectrum, wide_flux, narrow_flux, level):
    lines, rows, depth = spectrum.shape
    steps, groups = rows // BLOCK, lines // GROUP
    depth_high, depth_low = halves(cosine_matrix(depth))
    return pl.pallas_call(
        functools.partial(inverse_kernel, groups),
        grid=(steps + groups,),
        out_shape=jax.ShapeDtypeStruct((rows, lines, depth), jnp.float32),
        in_specs=[
            pl.BlockSpec((GROUP, rows, depth), lambda s: (jnp.minimum(s, groups - 1), 0, 0)),
            pl.BlockSpec((2, GROUP, depth), lambda s: (0, jnp.minimum(s, groups - 1), 0)),
            whole(2, rows, depth),
            whole(8, depth),
        ]
        + table_specs(rows, lines, depth),
        out_specs=pl.BlockSpec((BLOCK, lines, depth), lambda s: (jnp.maximum(s - groups, 0), 0, 0)),
        scratch_shapes=[pltpu.VMEM((depth // LANES, rows * lines, LANES), jnp.float32)],
        compiler_params=pltpu.CompilerParams(vmem_limit_bytes=VMEM_LIMIT),
    )(
        spectrum,
        wide_flux,
        narrow_flux,
        level,
        jnp.asarray(depth_high),
        jnp.asarray(depth_low),
        jnp.asarray(left_table(cosine_matrix(lines).T)),
        jnp.asarray(left_table(cosine_matrix(rows).T)),
        *box_tables(rows, lines, depth),
    )


def shards(slope_first, slope_second, slope_third):
    rows, lines, depth = slope_first.shape
    wide = lax.axis_size("wide")
    narrow = lax.axis_size("narrow")
    spectrum, wide_traces, narrow_traces = forward(slope_first, slope_second, slope_third)
    wide_flux, narrow_flux, level = exchange(wide_traces, narrow_traces, wide, narrow)
    return inverse(spectrum, wide_flux, narrow_flux, level)


def solution(mesh):
    placed = P("wide", "narrow", None)
    return jax.shard_map(shards, mesh=mesh, in_specs=(placed, placed, placed), out_specs=placed, check_vma=False)
```

```python
import functools
import math

import jax
import jax.numpy as jnp
import numpy as np
from jax import lax
from jax.experimental import pallas as pl
from jax.experimental.pallas import tpu as pltpu
from jax.sharding import PartitionSpec as P

HIGHEST = lax.Precision.HIGHEST


LANES = 128


def cosine_matrix(length):
    k = np.arange(length)[:, None]
    n = np.arange(length)[None, :]
    table = np.sqrt(2.0 / length) * np.cos(np.pi * ((2 * n + 1) * k % (4 * length)) / (2 * length))
    table[0] = np.sqrt(1.0 / length)
    return table


def sine_matrix(parts):
    m = np.arange(1, parts)
    return np.sqrt(2.0 / parts) * np.sin(np.pi * m[:, None] * m[None, :] / parts)


def modes(length):
    return 4.0 * np.sin(np.pi * np.arange(length) / (2 * length)) ** 2


def signs(length):
    return (-1.0) ** np.arange(length)


def face(length):
    return cosine_matrix(length)[:, 0]


def exponent(mu):
    return 2.0 * np.arcsinh(np.sqrt(mu) / 2.0)


def interface_gain(mu, cells, parts):
    kappa = exponent(mu)[..., None]
    angle = np.pi * np.arange(1, parts) / parts
    decay = np.exp(-kappa * cells)
    ratio = -np.expm1(-2.0 * kappa * cells) / (np.expm1(-kappa * cells) ** 2 + 2.0 * decay * (1.0 - np.cos(angle)))
    return np.tanh(kappa / 2.0) * ratio


def running_levels(parts):
    part = np.arange(parts)[:, None]
    step = np.arange(1, parts)[None, :]
    return (step <= part) - (parts - step) / parts


def bordered(matrix, top, left):
    return np.pad(matrix, ((top, 0), (left, 0)))


def lane_padded(table):
    pad = [(0, 0)] * (table.ndim - 1) + [(0, -table.shape[-1] % LANES)]
    return np.pad(table, pad)


@functools.lru_cache(None)
def tables(rows, lines, depth, wide, narrow):
    count = depth // (wide * narrow)
    row_modes, line_modes, depth_modes = modes(rows), modes(lines), modes(depth)
    row_face, line_face = face(rows), face(lines)
    own_all = np.eye(count)
    own_first = np.zeros((count, count))
    own_first[0, 0] = 1.0

    def over_narrow(matrix, own):
        return np.kron(np.eye(wide), np.kron(matrix, own))

    t = {}
    t["sine"] = over_narrow(bordered(sine_matrix(narrow), 1, 1), own_all)
    levels = running_levels(narrow)
    steady = np.cumsum(-levels / line_face[0], axis=0)[:-1] / line_face[0]
    t["steady"] = over_narrow(bordered(steady, 1, 1), own_first)
    balance = -(row_face[0] / line_face[0]) * np.tril(np.ones((narrow - 1, narrow)))
    t["balance"] = over_narrow(bordered(balance, 1, 0), own_first)
    k = np.arange(1, lines)
    near = np.sum(line_face[k] ** 2 / line_modes[k])
    far = np.sum(signs(lines)[k] * line_face[k] ** 2 / line_modes[k])
    link = (1.0 + 2.0 * near) * np.eye(narrow - 1) - far * (np.eye(narrow - 1, k=1) + np.eye(narrow - 1, k=-1))
    t["level_flux"] = over_narrow(bordered(levels @ link / line_face[0], 0, 1), own_first)
    t["level_jump"] = over_narrow(bordered(-levels / line_face[0], 0, 1), own_first)
    level_wide = bordered(-running_levels(wide) / (row_face[0] * math.sqrt(narrow)), 0, 1)
    first_column = np.zeros((count, 1))
    first_column[0, 0] = 1.0
    t["level_wide"] = np.kron(first_column.T, np.kron(level_wide, np.kron(np.ones((narrow, 1)), first_column)))
    gain = interface_gain(depth_modes[:, None] + row_modes[None, :], lines, narrow)
    gain[0, 0, :] = 0.0
    gain = bordered(np.moveaxis(gain, 2, 1).reshape(depth * (narrow - 1), rows), 0, 0)
    gain = np.pad(gain.reshape(depth, narrow - 1, rows), ((0, 0), (1, 0), (0, 0)))
    gain = gain.reshape(wide * narrow, count, narrow, rows).swapaxes(1, 2)
    t["gain"] = lane_padded(gain.reshape(wide * narrow, narrow * count, rows))
    full = cosine_matrix(lines * narrow).reshape(lines * narrow, narrow, lines)
    join = np.einsum("qJn,kn->Jkq", full, cosine_matrix(lines))
    t["join_high"], t["join_low"] = halves(join)
    t["part_high"], t["part_low"] = halves(np.swapaxes(join, 1, 2))
    shift = depth_modes[:, None] + modes(lines * narrow)[None, :]
    decay = np.expm1(-exponent(shift) * rows)
    top = -np.sqrt(shift / (4.0 + shift)) * decay * (2.0 + decay)
    t["decay"] = np.stack([decay, top], axis=1).reshape(-1, 8, lines * narrow)
    t["wide_sine"] = np.kron(own_all, bordered(sine_matrix(wide), 1, 1))
    angle = 1.0 - np.cos(np.pi * np.arange(wide) / wide)
    angle[0] = 1.0
    t["angle"] = np.broadcast_to(angle[:, None], (wide, lines * narrow))
    t["box_modes"] = row_modes[:, None] + line_modes[None, :]
    both = row_face[:, None] * line_face[None, :]
    t["faces"] = np.stack([both, both * signs(rows)[:, None]])
    t["box_modes_turned"] = t["box_modes"].T
    t["faces_turned"] = np.stack([both.T, both.T * signs(lines)[:, None]])
    t["alternate"] = np.broadcast_to(signs(LANES)[None, :], (8, LANES))
    return {
        name: np.ascontiguousarray(value, dtype=jnp.bfloat16 if name[:4] in ("join", "part") else np.float32)
        for name, value in t.items()
    }


FIXED = (
    "sine",
    "steady",
    "balance",
    "level_flux",
    "level_jump",
    "level_wide",
    "join_high",
    "join_low",
    "part_high",
    "part_low",
    "wide_sine",
    "angle",
    "box_modes",
    "faces",
    "box_modes_turned",
    "faces_turned",
    "alternate",
)


def halves(table):
    table = np.asarray(table, np.float32)
    high = table.astype(jnp.bfloat16)
    low = (table - high.astype(np.float32)).astype(jnp.bfloat16)
    return high, low


def left_table(table):
    high, low = halves(table)
    return np.block([[high, high], [low, np.zeros_like(low)]])


def split(x):
    high = x.astype(jnp.bfloat16)
    return high, (x - high.astype(jnp.float32)).astype(jnp.bfloat16)


def dot(a, b):
    return jnp.dot(a, b, preferred_element_type=jnp.float32)


def from_left(table, x):
    both = dot(table, jnp.concatenate(split(x), axis=0))
    count = x.shape[0]
    return both[:count] + both[count:]


def from_right(x, high_table, low_table):
    high, low = split(x)
    return dot(high, high_table) + dot(low, high_table) + dot(high, low_table)


def lower_neighbour(x, axis):
    index = lax.broadcasted_iota(jnp.int32, x.shape, axis)
    x = jnp.where(index < x.shape[axis] - 1, x, 0.0)
    return pltpu.roll(x, 1, axis) - x


def put(held, where, value):
    for panel in range(held.shape[0]):
        held[panel, where, :] = value[:, panel * LANES : (panel + 1) * LANES]


def take(held, where):
    return jnp.concatenate([held[panel, where, :] for panel in range(held.shape[0])], axis=1)


def forward_kernel(
    steps,
    first_ref,
    second_ref,
    third_ref,
    depth_high_ref,
    depth_low_ref,
    line_ref,
    row_ref,
    shift_ref,
    faces_ref,
    line_shift_ref,
    line_face_ref,
    out_ref,
    wide_ref,
    narrow_ref,
    carry,
    held,
    wide_face,
    narrow_face,
):
    step = pl.program_id(0)
    rows, lines = row_ref.shape[0] // 2, line_ref.shape[0] // 2
    block = first_ref.shape[0]
    group = out_ref.shape[0]

    @pl.when(step == 0)
    def _():
        carry[...] = jnp.zeros_like(carry)

    @pl.when(step < steps)
    def _():
        below = carry[...]
        parts = []
        for i in range(block):
            here = first_ref[i]
            if i == block - 1:
                here = jnp.where(step < steps - 1, here, 0.0)
            part = below - here + lower_neighbour(second_ref[i], 0) + lower_neighbour(third_ref[i], 1)
            below = here
            parts.append(part)
            narrow_face[pl.ds(step * block + i, 1), :] = second_ref[i, lines - 1 : lines, :]
        carry[...] = below
        stacked = from_right(jnp.concatenate(parts, axis=0), depth_high_ref[...], depth_low_ref[...])
        for i in range(block):
            part = from_left(line_ref[...], stacked[i * lines : (i + 1) * lines])
            put(held, pl.ds(pl.multiple_of((step * block + i) * lines, 8), lines), part)

    @pl.when(step == steps)
    def _():
        face = from_right(first_ref[block - 1], depth_high_ref[...], depth_low_ref[...])
        wide_face[...] = from_left(line_ref[...], face)
        face = from_right(narrow_face[...], depth_high_ref[...], depth_low_ref[...])
        narrow_ref[0] = jnp.zeros_like(face)
        narrow_ref[1] = from_left(row_ref[...], face)

    @pl.when(step >= steps)
    def _():
        lows, highs = [], []
        narrow_low, narrow_high = narrow_ref[0], narrow_ref[1]
        for i in range(group):
            line = (step - steps) * group + i
            part = from_left(row_ref[...], take(held, pl.ds(line, rows, stride=lines)))
            out_ref[i] = part
            eig = shift_ref[...] + line_shift_ref[line]
            closed = jnp.where(eig > 0.0, part / eig, 0.0)
            lows.append(jnp.sum(closed * faces_ref[0], axis=0, keepdims=True))
            highs.append(jnp.sum(closed * faces_ref[1], axis=0, keepdims=True))
            closed = closed * line_face_ref[line]
            narrow_low = narrow_low + closed
            narrow_high = narrow_high + closed if i % 2 == 0 else narrow_high - closed
        here = pl.ds(pl.multiple_of((step - steps) * group, 8), group)
        wide_ref[0, here, :] = jnp.concatenate(lows, axis=0)
        wide_ref[1, here, :] = jnp.concatenate(highs, axis=0) + wide_face[here, :]
        narrow_ref[0] = narrow_low
        narrow_ref[1] = narrow_high


def inverse_kernel(
    steps,
    spectrum_ref,
    wide_ref,
    narrow_ref,
    level_ref,
    depth_high_ref,
    depth_low_ref,
    line_ref,
    row_ref,
    shift_ref,
    faces_ref,
    line_shift_ref,
    line_face_ref,
    out_ref,
    held,
):
    step = pl.program_id(0)
    rows, lines = row_ref.shape[0] // 2, line_ref.shape[0] // 2
    block = out_ref.shape[0]
    group = spectrum_ref.shape[0]

    @pl.when(step < steps)
    def _():
        for i in range(group):
            line = step * group + i
            added = faces_ref[1] * wide_ref[1, i : i + 1, :] - faces_ref[0] * wide_ref[0, i : i + 1, :]
            turned = narrow_ref[1] if i % 2 == 0 else -narrow_ref[1]
            part = spectrum_ref[i] + added + line_face_ref[line] * (turned - narrow_ref[0])
            eig = shift_ref[...] + line_shift_ref[line]
            part = jnp.where(eig > 0.0, part / eig, level_ref[:1])
            put(held, pl.ds(line, rows, stride=lines), from_left(row_ref[...], part))

    @pl.when(step >= steps)
    def _():
        parts = []
        for i in range(block):
            here = pl.multiple_of(((step - steps) * block + i) * lines, 8)
            parts.append(from_left(line_ref[...], take(held, pl.ds(here, lines))))
        result = from_right(jnp.concatenate(parts, axis=0), depth_high_ref[...], depth_low_ref[...])
        for i in range(block):
            out_ref[i] = result[i * lines : (i + 1) * lines]


MESH = pl.DeviceIdType.MESH


def greet(wide, narrow):
    w, n = lax.axis_index("wide"), lax.axis_index("narrow")
    barrier = pltpu.get_barrier_semaphore()
    for d in range(1, narrow):
        pl.semaphore_signal(barrier, inc=1, device_id=(w, lax.rem(n + d, narrow)), device_id_type=MESH)
    for d in range(1, wide):
        pl.semaphore_signal(barrier, inc=1, device_id=(lax.rem(w + d, wide), n), device_id_type=MESH)


def trade(axis, source, target, send, recv):
    w, n = lax.axis_index("wide"), lax.axis_index("narrow")
    peers = source.shape[0]
    here = w if axis == "wide" else n
    copies = []
    for d in range(1, peers):
        to = lax.rem(here + d, peers)
        copies.append(
            pltpu.make_async_remote_copy(
                src_ref=source.at[to],
                dst_ref=target.at[here],
                send_sem=send.at[d],
                recv_sem=recv.at[d],
                device_id=(to, n) if axis == "wide" else (w, to),
                device_id_type=MESH,
            )
        )
    for copy in copies:
        copy.start()
    target[here] = source[here]
    for copy in copies:
        copy.wait()


def turn(source, target):
    outer = source.shape[0]
    inner = target.shape[0]
    count = source.shape[1] // inner
    for a in range(outer):
        for b in range(inner):
            target[b, a * count : (a + 1) * count, :] = source[a, b * count : (b + 1) * count, :]


def exact(a, b):
    return jnp.dot(a, b, precision=HIGHEST, preferred_element_type=jnp.float32)


def interfaces(traces, t, gain, decay, modes_ref, place, jumps, fluxes, wide, narrow):
    total = traces.shape[0]
    count = total // (wide * narrow)
    span = narrow * count
    rows, lines = t["box_modes"].shape
    row = lax.broadcasted_iota(jnp.int32, (total, 1), 0)
    has_wide = row >= span
    has_narrow = (row & (span - 1)) >= count
    own_mode = row & (count - 1)
    holds_steady = place == 0

    def up(x, by):
        return pltpu.roll(x, total - by, 0)

    def by_mode(x, weights):
        out = exact(x, weights[0])
        for mode in range(1, count):
            out = jnp.where(own_mode == mode, exact(x, weights[mode]), out)
        return out

    def influence(box_modes, faces, side, first):
        weights = []
        low = lax.broadcasted_iota(jnp.int32, box_modes.shape, 0) == 0
        left = lax.broadcasted_iota(jnp.int32, box_modes.shape, 1) == 0
        for mode in range(count):
            shift = modes_ref[place * count + mode]
            eig = box_modes[...] + shift
            some = eig > 0.0
            value = jnp.where(some, faces[side] / eig, faces[side] if first else 0.0)
            if first and mode == 0:
                value = jnp.where(low & jnp.logical_not(left) & holds_steady, 0.0, value)
            weights.append(value)
        return weights

    alternate = t["alternate"][:1, :]
    wide_low, wide_high = traces[:, :lines], traces[:, LANES : LANES + lines]
    narrow_low, narrow_high = traces[:, 2 * LANES : 2 * LANES + rows], traces[:, 2 * LANES + rows : 2 * LANES + 2 * rows]
    jump_narrow = jnp.where(has_narrow, narrow_low - pltpu.roll(narrow_high, count, 0), 0.0)
    jump_wide = jnp.where(has_wide, wide_low - pltpu.roll(wide_high, span, 0), 0.0)
    gain = jnp.concatenate([gain[:, :rows]] * wide, axis=0)
    sine = t["sine"][...]

    def glued(jump):
        return exact(sine, gain * exact(sine, jump))

    row_zero = lax.broadcasted_iota(jnp.int32, (total, rows), 1) == 0
    flux = glued(jump_narrow)
    steady = exact(t["steady"][...], jump_narrow)
    flux = flux + jnp.where(row_zero & holds_steady, steady, 0.0)
    moved = []
    for side in range(2):
        value = by_mode(flux, influence(t["box_modes"], t["faces"], side, True))
        moved.append(alternate[:, :lines] * up(value, count) - value)
    jump_wide = jump_wide + jnp.where(has_wide, moved[0] - pltpu.roll(moved[1], span, 0), 0.0)
    pad = jnp.zeros((total, LANES - lines), jnp.float32)
    jumps[...] = jnp.concatenate([jump_wide, pad], axis=1)
    joined = jnp.zeros((count * wide, lines * narrow), jnp.float32)
    for J in range(narrow):
        part = [jumps[pl.ds(J * count + mode, wide, stride=span), :] for mode in range(count)]
        joined = joined + from_right(
            jnp.concatenate(part, axis=0)[:, :lines], t["join_high"][J], t["join_low"][J]
        )
    wide_gain = []
    for mode in range(count):
        at, top = decay[2 * mode : 2 * mode + 1], decay[2 * mode + 1 : 2 * mode + 2]
        wide_gain.append(top / (at * at + 2.0 * (1.0 + at) * t["angle"][...]))
    wide_sine = t["wide_sine"][...]
    shaped = exact(wide_sine, jnp.concatenate(wide_gain, axis=0) * exact(wide_sine, joined))
    pad = jnp.zeros((wide, LANES - lines), jnp.float32)
    for J in range(narrow):
        part = from_right(shaped, t["part_high"][J], t["part_low"][J])
        for mode in range(count):
            fluxes[pl.ds(J * count + mode, wide, stride=span), :] = jnp.concatenate(
                [part[mode * wide : (mode + 1) * wide], pad], axis=1
            )
    padded_wide = fluxes[...]
    flux_wide = padded_wide[:, :lines]
    moved = []
    for side in range(2):
        value = by_mode(flux_wide, influence(t["box_modes_turned"], t["faces_turned"], side, False))
        moved.append(alternate[:, :rows] * up(value, span) - value)
    jump_narrow = jump_narrow + jnp.where(has_narrow, moved[0] - pltpu.roll(moved[1], count, 0), 0.0)
    flux_narrow = glued(jump_narrow)
    padded_high = up(padded_wide, span)
    balanced = exact(t["balance"][...], (padded_high - padded_wide)[:, :rows])
    level = exact(t["level_flux"][...], balanced) + exact(t["level_jump"][...], jump_narrow)
    level = level + exact(t["level_wide"][...], joined[:, :rows])
    flux_narrow = jnp.where(row_zero & (own_mode == 0) & holds_steady, balanced, flux_narrow)
    rest = level[:, : LANES - 2 * rows]
    return jnp.concatenate([padded_wide, padded_high, flux_narrow, up(flux_narrow, count), rest], axis=1)


def forward_exchange_kernel(steps, groups, wide, narrow, *refs):
    step = pl.program_id(0)
    names = len(FIXED)
    box_in, refs = refs[:11], refs[11:]
    sources, gain_hbm, decay_hbm, modes_ref = refs[:names], refs[names], refs[names + 1], refs[names + 2]
    spectrum_ref, wide_ref, narrow_ref, level_ref = refs[names + 3 : names + 7]
    refs = refs[names + 7 :]
    carry, held, wide_face, narrow_face, wide_in, narrow_in = refs[:6]
    fixed, refs = refs[6 : 6 + names], refs[6 + names :]
    gain, decay, near_a, near_b, far_a, far_b, near_c, far_c, jumps, fluxes = refs[:10]
    table_sem, near_send, near_recv, far_send, far_recv, near_send2, near_recv2, far_send2, far_recv2 = refs[10:]
    lines, depth = wide_in.shape[1:]
    rows = narrow_in.shape[1]
    count = depth // (wide * narrow)
    place = lax.axis_index("narrow") * wide + lax.axis_index("wide")
    per_block = 8 // (2 * count)
    own = [(gain_hbm.at[place], gain), (decay_hbm.at[lax.div(place, per_block)], decay)]
    pairs = list(zip(sources, fixed)) + own

    @pl.when(step == 0)
    def _():
        greet(wide, narrow)
        for copy in prepared(pairs, table_sem):
            copy.start()

    forward_kernel(steps, *box_in, spectrum_ref, wide_in, narrow_in, carry, held, wide_face, narrow_face)

    @pl.when(step == steps + groups - 1)
    def _():
        gap = jnp.zeros((LANES - lines, depth), jnp.float32)
        rest = jnp.zeros((LANES - 2 * rows, depth), jnp.float32)
        values = jnp.concatenate([wide_in[0], gap, wide_in[1], gap, narrow_in[0], narrow_in[1], rest], axis=0).T
        far_rows = wide * count
        for p in range(narrow):
            near_a[p] = values[p * far_rows : (p + 1) * far_rows]
        pl.semaphore_wait(pltpu.get_barrier_semaphore(), wide + narrow - 2)
        trade("narrow", near_a, near_b, near_send, near_recv)
        turn(near_b, far_a)
        trade("wide", far_a, far_b, far_send, far_recv)
        for copy in prepared(pairs, table_sem):
            copy.wait()
        traces = jnp.concatenate([far_b[p] for p in range(wide)], axis=0)
        here = lax.rem(place, per_block)
        own_decay = decay[: 2 * count]
        for p in range(1, per_block):
            own_decay = jnp.where(here == p, decay[p * 2 * count : (p + 1) * 2 * count], own_decay)
        table = dict(zip(FIXED, fixed))
        out = interfaces(traces, table, gain[...], own_decay, modes_ref, place, jumps, fluxes, wide, narrow)
        span = narrow * count
        for p in range(wide):
            far_a[p] = out[p * span : (p + 1) * span]
        trade("wide", far_a, far_c, far_send2, far_recv2)
        turn(far_c, near_a)
        trade("narrow", near_a, near_c, near_send2, near_recv2)
        values = jnp.concatenate([near_c[p] for p in range(narrow)], axis=0).T
        wide_ref[0] = values[:lines]
        wide_ref[1] = values[LANES : LANES + lines]
        narrow_ref[0] = values[2 * LANES : 2 * LANES + rows]
        narrow_ref[1] = values[2 * LANES + rows : 2 * LANES + 2 * rows]
        level_ref[...] = values[2 * (LANES + rows) : 2 * (LANES + rows) + 8]


def prepared(pairs, sem):
    return [pltpu.make_async_copy(source, target, sem.at[i]) for i, (source, target) in enumerate(pairs)]


IN_VMEM = pl.BlockSpec(memory_space=pltpu.VMEM)
IN_HBM = pl.BlockSpec(memory_space=pl.ANY)
IN_SMEM = pl.BlockSpec(memory_space=pltpu.SMEM)


VMEM_LIMIT = 60 * 2**20
BLOCK = 16
GROUP = 16


def box_tables(rows, lines, depth):
    shift = modes(rows)[:, None] + modes(depth)[None, :]
    low = np.broadcast_to(face(rows)[:, None], (rows, depth))
    high = np.broadcast_to((face(rows) * signs(rows))[:, None], (rows, depth))
    faces = np.stack([low, high])
    return [jnp.asarray(v, jnp.float32) for v in (shift, faces, modes(lines), face(lines))]


def whole(*shape):
    return pl.BlockSpec(shape, lambda s: (0,) * len(shape))


def table_specs(rows, lines, depth):
    return [
        whole(depth, depth),
        whole(depth, depth),
        whole(2 * lines, 2 * lines),
        whole(2 * rows, 2 * rows),
        whole(rows, depth),
        whole(2, rows, depth),
        pl.BlockSpec(memory_space=pltpu.SMEM),
        pl.BlockSpec(memory_space=pltpu.SMEM),
    ]


def forward_exchange(first, second, third, wide, narrow):
    rows, lines, depth = first.shape
    steps, groups = rows // BLOCK, lines // GROUP
    count = depth // (wide * narrow)
    slab = pl.BlockSpec((BLOCK, lines, depth), lambda s: (jnp.minimum(s, steps - 1), 0, 0))
    depth_high, depth_low = halves(cosine_matrix(depth).T)
    t = tables(rows, lines, depth, wide, narrow)
    width = 3 * LANES
    near = (narrow, wide * count, width)
    far = (wide, narrow * count, width)
    face_rows = (wide * narrow * count, LANES)
    f32 = jnp.float32
    fixed = [jnp.asarray(t[name]) for name in FIXED]
    box_shapes = [
        (lines, depth),
        (depth // LANES, rows * lines, LANES),
        (lines, depth),
        (rows, depth),
        (2, lines, depth),
        (2, rows, depth),
    ]
    shapes = [t["gain"].shape[1:], t["decay"].shape[1:], near, near, far, far, near, far, face_rows, face_rows]
    sems = [len(fixed) + 2, narrow, narrow, wide, wide, narrow, narrow, wide, wide]
    return pl.pallas_call(
        functools.partial(forward_exchange_kernel, steps, groups, wide, narrow),
        grid=(steps + groups,),
        out_shape=[
            jax.ShapeDtypeStruct((lines, rows, depth), f32),
            jax.ShapeDtypeStruct((2, lines, depth), f32),
            jax.ShapeDtypeStruct((2, rows, depth), f32),
            jax.ShapeDtypeStruct((8, depth), f32),
        ],
        in_specs=[slab, slab, slab]
        + table_specs(rows, lines, depth)
        + [IN_HBM] * (len(fixed) + 2)
        + [IN_SMEM],
        out_specs=[
            pl.BlockSpec((GROUP, rows, depth), lambda s: (jnp.maximum(s - steps, 0), 0, 0)),
            whole(2, lines, depth),
            whole(2, rows, depth),
            whole(8, depth),
        ],
        scratch_shapes=[pltpu.VMEM(v, f32) for v in box_shapes]
        + [pltpu.VMEM(v.shape, v.dtype) for v in fixed]
        + [pltpu.VMEM(v, f32) for v in shapes]
        + [pltpu.SemaphoreType.DMA((k,)) for k in sems],
        compiler_params=pltpu.CompilerParams(
            collective_id=0, has_side_effects=True, vmem_limit_bytes=VMEM_LIMIT
        ),
    )(
        first,
        second,
        third,
        jnp.asarray(depth_high),
        jnp.asarray(depth_low),
        jnp.asarray(left_table(cosine_matrix(lines))),
        jnp.asarray(left_table(cosine_matrix(rows))),
        *box_tables(rows, lines, depth),
        *fixed,
        jnp.asarray(t["gain"]),
        jnp.asarray(t["decay"]),
        jnp.asarray(modes(depth), f32),
    )


def inverse(spectrum, wide_flux, narrow_flux, level):
    lines, rows, depth = spectrum.shape
    steps, groups = rows // BLOCK, lines // GROUP
    depth_high, depth_low = halves(cosine_matrix(depth))
    return pl.pallas_call(
        functools.partial(inverse_kernel, groups),
        grid=(steps + groups,),
        out_shape=jax.ShapeDtypeStruct((rows, lines, depth), jnp.float32),
        in_specs=[
            pl.BlockSpec((GROUP, rows, depth), lambda s: (jnp.minimum(s, groups - 1), 0, 0)),
            pl.BlockSpec((2, GROUP, depth), lambda s: (0, jnp.minimum(s, groups - 1), 0)),
            whole(2, rows, depth),
            whole(8, depth),
        ]
        + table_specs(rows, lines, depth),
        out_specs=pl.BlockSpec((BLOCK, lines, depth), lambda s: (jnp.maximum(s - groups, 0), 0, 0)),
        scratch_shapes=[pltpu.VMEM((depth // LANES, rows * lines, LANES), jnp.float32)],
        compiler_params=pltpu.CompilerParams(vmem_limit_bytes=VMEM_LIMIT),
    )(
        spectrum,
        wide_flux,
        narrow_flux,
        level,
        jnp.asarray(depth_high),
        jnp.asarray(depth_low),
        jnp.asarray(left_table(cosine_matrix(lines).T)),
        jnp.asarray(left_table(cosine_matrix(rows).T)),
        *box_tables(rows, lines, depth),
    )


def shards(slope_first, slope_second, slope_third):
    rows, lines, depth = slope_first.shape
    wide = lax.axis_size("wide")
    narrow = lax.axis_size("narrow")
    spectrum, wide_flux, narrow_flux, level = forward_exchange(slope_first, slope_second, slope_third, wide, narrow)
    return inverse(spectrum, wide_flux, narrow_flux, level)


def solution(mesh):
    placed = P("wide", "narrow", None)
    return jax.shard_map(shards, mesh=mesh, in_specs=(placed, placed, placed), out_specs=placed, check_vma=False)
```

```python
import functools
import math

import jax
import jax.numpy as jnp
import numpy as np
from jax import lax
from jax.experimental import pallas as pl
from jax.experimental.pallas import tpu as pltpu
from jax.sharding import PartitionSpec as P

HIGHEST = lax.Precision.HIGHEST


LANES = 128


def cosine_matrix(length):
    k = np.arange(length)[:, None]
    n = np.arange(length)[None, :]
    table = np.sqrt(2.0 / length) * np.cos(np.pi * ((2 * n + 1) * k % (4 * length)) / (2 * length))
    table[0] = np.sqrt(1.0 / length)
    return table


def sine_matrix(parts):
    m = np.arange(1, parts)
    return np.sqrt(2.0 / parts) * np.sin(np.pi * m[:, None] * m[None, :] / parts)


def modes(length):
    return 4.0 * np.sin(np.pi * np.arange(length) / (2 * length)) ** 2


def signs(length):
    return (-1.0) ** np.arange(length)


def face(length):
    return cosine_matrix(length)[:, 0]


def exponent(mu):
    return 2.0 * np.arcsinh(np.sqrt(mu) / 2.0)


def interface_gain(mu, cells, parts):
    kappa = exponent(mu)[..., None]
    angle = np.pi * np.arange(1, parts) / parts
    decay = np.exp(-kappa * cells)
    ratio = -np.expm1(-2.0 * kappa * cells) / (np.expm1(-kappa * cells) ** 2 + 2.0 * decay * (1.0 - np.cos(angle)))
    return np.tanh(kappa / 2.0) * ratio


def running_levels(parts):
    part = np.arange(parts)[:, None]
    step = np.arange(1, parts)[None, :]
    return (step <= part) - (parts - step) / parts


def bordered(matrix, top, left):
    return np.pad(matrix, ((top, 0), (left, 0)))


def lane_padded(table):
    pad = [(0, 0)] * (table.ndim - 1) + [(0, -table.shape[-1] % LANES)]
    return np.pad(table, pad)


@functools.lru_cache(None)
def tables(rows, lines, depth, wide, narrow):
    count = depth // (wide * narrow)
    row_modes, line_modes, depth_modes = modes(rows), modes(lines), modes(depth)
    row_face, line_face = face(rows), face(lines)
    own_all = np.eye(count)
    own_first = np.zeros((count, count))
    own_first[0, 0] = 1.0

    def over_narrow(matrix, own):
        return np.kron(np.eye(wide), np.kron(matrix, own))

    t = {}
    t["sine"] = over_narrow(bordered(sine_matrix(narrow), 1, 1), own_all)
    levels = running_levels(narrow)
    steady = np.cumsum(-levels / line_face[0], axis=0)[:-1] / line_face[0]
    t["steady"] = over_narrow(bordered(steady, 1, 1), own_first)
    balance = -(row_face[0] / line_face[0]) * np.tril(np.ones((narrow - 1, narrow)))
    t["balance"] = over_narrow(bordered(balance, 1, 0), own_first)
    k = np.arange(1, lines)
    near = np.sum(line_face[k] ** 2 / line_modes[k])
    far = np.sum(signs(lines)[k] * line_face[k] ** 2 / line_modes[k])
    link = (1.0 + 2.0 * near) * np.eye(narrow - 1) - far * (np.eye(narrow - 1, k=1) + np.eye(narrow - 1, k=-1))
    t["level_flux"] = over_narrow(bordered(levels @ link / line_face[0], 0, 1), own_first)
    t["level_jump"] = over_narrow(bordered(-levels / line_face[0], 0, 1), own_first)
    level_wide = bordered(-running_levels(wide) / (row_face[0] * math.sqrt(narrow)), 0, 1)
    first_column = np.zeros((count, 1))
    first_column[0, 0] = 1.0
    t["level_wide"] = np.kron(first_column.T, np.kron(level_wide, np.kron(np.ones((narrow, 1)), first_column)))
    gain = interface_gain(depth_modes[:, None] + row_modes[None, :], lines, narrow)
    gain[0, 0, :] = 0.0
    gain = bordered(np.moveaxis(gain, 2, 1).reshape(depth * (narrow - 1), rows), 0, 0)
    gain = np.pad(gain.reshape(depth, narrow - 1, rows), ((0, 0), (1, 0), (0, 0)))
    gain = gain.reshape(wide * narrow, count, narrow, rows).swapaxes(1, 2)
    t["gain"] = lane_padded(gain.reshape(wide * narrow, narrow * count, rows))
    full = cosine_matrix(lines * narrow).reshape(lines * narrow, narrow, lines)
    join = np.einsum("qJn,kn->Jkq", full, cosine_matrix(lines))
    t["join_high"], t["join_low"] = halves(join)
    t["part_high"], t["part_low"] = halves(np.swapaxes(join, 1, 2))
    shift = depth_modes[:, None] + modes(lines * narrow)[None, :]
    decay = np.expm1(-exponent(shift) * rows)
    top = -np.sqrt(shift / (4.0 + shift)) * decay * (2.0 + decay)
    t["decay"] = np.stack([decay, top], axis=1).reshape(-1, 8, lines * narrow)
    t["wide_sine"] = np.kron(own_all, bordered(sine_matrix(wide), 1, 1))
    angle = 1.0 - np.cos(np.pi * np.arange(wide) / wide)
    angle[0] = 1.0
    t["angle"] = np.broadcast_to(angle[:, None], (wide, lines * narrow))
    t["box_modes"] = row_modes[:, None] + line_modes[None, :]
    both = row_face[:, None] * line_face[None, :]
    t["faces"] = np.stack([both, both * signs(rows)[:, None]])
    t["box_modes_turned"] = t["box_modes"].T
    t["faces_turned"] = np.stack([both.T, both.T * signs(lines)[:, None]])
    t["alternate"] = np.broadcast_to(signs(LANES)[None, :], (8, LANES))
    return {
        name: np.ascontiguousarray(value, dtype=jnp.bfloat16 if name[:4] in ("join", "part") else np.float32)
        for name, value in t.items()
    }


FIXED = (
    "sine",
    "steady",
    "balance",
    "level_flux",
    "level_jump",
    "level_wide",
    "join_high",
    "join_low",
    "part_high",
    "part_low",
    "wide_sine",
    "angle",
    "box_modes",
    "faces",
    "box_modes_turned",
    "faces_turned",
    "alternate",
)


def halves(table):
    table = np.asarray(table, np.float32)
    high = table.astype(jnp.bfloat16)
    low = (table - high.astype(np.float32)).astype(jnp.bfloat16)
    return high, low


def left_table(table):
    high, low = halves(table)
    return np.block([[high, high], [low, np.zeros_like(low)]])


def split(x):
    high = x.astype(jnp.bfloat16)
    return high, (x - high.astype(jnp.float32)).astype(jnp.bfloat16)


def dot(a, b):
    return jnp.dot(a, b, preferred_element_type=jnp.float32)


def from_left(table, x):
    both = dot(table, jnp.concatenate(split(x), axis=0))
    count = x.shape[0]
    return both[:count] + both[count:]


def from_right(x, high_table, low_table):
    high, low = split(x)
    return dot(high, high_table) + dot(low, high_table) + dot(high, low_table)


def lower_neighbour(x, axis):
    index = lax.broadcasted_iota(jnp.int32, x.shape, axis)
    x = jnp.where(index < x.shape[axis] - 1, x, 0.0)
    return pltpu.roll(x, 1, axis) - x


def put(held, where, value):
    for panel in range(held.shape[0]):
        held[panel, where, :] = value[:, panel * LANES : (panel + 1) * LANES]


def take(held, where):
    return jnp.concatenate([held[panel, where, :] for panel in range(held.shape[0])], axis=1)


def forward_kernel(
    steps,
    first_ref,
    second_ref,
    third_ref,
    depth_high_ref,
    depth_low_ref,
    line_ref,
    row_ref,
    shift_ref,
    faces_ref,
    line_shift_ref,
    line_face_ref,
    out_ref,
    wide_ref,
    narrow_ref,
    carry,
    held,
    wide_face,
    narrow_face,
):
    step = pl.program_id(0)
    rows, lines = row_ref.shape[0] // 2, line_ref.shape[0] // 2
    block = first_ref.shape[0]
    group = out_ref.shape[0]

    @pl.when(step == 0)
    def _():
        carry[...] = jnp.zeros_like(carry)

    @pl.when(step < steps)
    def _():
        below = carry[...]
        parts = []
        for i in range(block):
            here = first_ref[i]
            if i == block - 1:
                here = jnp.where(step < steps - 1, here, 0.0)
            part = below - here + lower_neighbour(second_ref[i], 0) + lower_neighbour(third_ref[i], 1)
            below = here
            parts.append(part)
            narrow_face[pl.ds(step * block + i, 1), :] = second_ref[i, lines - 1 : lines, :]
        carry[...] = below
        stacked = from_right(jnp.concatenate(parts, axis=0), depth_high_ref[...], depth_low_ref[...])
        for i in range(block):
            part = from_left(line_ref[...], stacked[i * lines : (i + 1) * lines])
            put(held, pl.ds(pl.multiple_of((step * block + i) * lines, 8), lines), part)

    @pl.when(step == steps)
    def _():
        face = from_right(first_ref[block - 1], depth_high_ref[...], depth_low_ref[...])
        wide_face[...] = from_left(line_ref[...], face)
        face = from_right(narrow_face[...], depth_high_ref[...], depth_low_ref[...])
        narrow_ref[0] = jnp.zeros_like(face)
        narrow_ref[1] = from_left(row_ref[...], face)

    @pl.when(step >= steps)
    def _():
        lows, highs = [], []
        narrow_low, narrow_high = narrow_ref[0], narrow_ref[1]
        for i in range(group):
            line = (step - steps) * group + i
            part = from_left(row_ref[...], take(held, pl.ds(line, rows, stride=lines)))
            out_ref[i] = part
            eig = shift_ref[...] + line_shift_ref[line]
            closed = jnp.where(eig > 0.0, part / eig, 0.0)
            lows.append(jnp.sum(closed * faces_ref[0], axis=0, keepdims=True))
            highs.append(jnp.sum(closed * faces_ref[1], axis=0, keepdims=True))
            closed = closed * line_face_ref[line]
            narrow_low = narrow_low + closed
            narrow_high = narrow_high + closed if i % 2 == 0 else narrow_high - closed
        here = pl.ds(pl.multiple_of((step - steps) * group, 8), group)
        wide_ref[0, here, :] = jnp.concatenate(lows, axis=0)
        wide_ref[1, here, :] = jnp.concatenate(highs, axis=0) + wide_face[here, :]
        narrow_ref[0] = narrow_low
        narrow_ref[1] = narrow_high


def inverse_kernel(
    steps,
    spectrum_ref,
    wide_ref,
    narrow_ref,
    level_ref,
    depth_high_ref,
    depth_low_ref,
    line_ref,
    row_ref,
    shift_ref,
    faces_ref,
    line_shift_ref,
    line_face_ref,
    out_ref,
    held,
):
    step = pl.program_id(0)
    rows, lines = row_ref.shape[0] // 2, line_ref.shape[0] // 2
    block = out_ref.shape[0]
    group = spectrum_ref.shape[0]

    @pl.when(step < steps)
    def _():
        for i in range(group):
            line = step * group + i
            added = faces_ref[1] * wide_ref[1, i : i + 1, :] - faces_ref[0] * wide_ref[0, i : i + 1, :]
            turned = narrow_ref[1] if i % 2 == 0 else -narrow_ref[1]
            part = spectrum_ref[i] + added + line_face_ref[line] * (turned - narrow_ref[0])
            eig = shift_ref[...] + line_shift_ref[line]
            part = jnp.where(eig > 0.0, part / eig, level_ref[:1])
            put(held, pl.ds(line, rows, stride=lines), from_left(row_ref[...], part))

    @pl.when(step >= steps)
    def _():
        parts = []
        for i in range(block):
            here = pl.multiple_of(((step - steps) * block + i) * lines, 8)
            parts.append(from_left(line_ref[...], take(held, pl.ds(here, lines))))
        result = from_right(jnp.concatenate(parts, axis=0), depth_high_ref[...], depth_low_ref[...])
        for i in range(block):
            out_ref[i] = result[i * lines : (i + 1) * lines]


MESH = pl.DeviceIdType.MESH


def greet(wide, narrow):
    w, n = lax.axis_index("wide"), lax.axis_index("narrow")
    barrier = pltpu.get_barrier_semaphore()
    for d in range(1, narrow):
        pl.semaphore_signal(barrier, inc=1, device_id=(w, lax.rem(n + d, narrow)), device_id_type=MESH)
    for d in range(1, wide):
        pl.semaphore_signal(barrier, inc=1, device_id=(lax.rem(w + d, wide), n), device_id_type=MESH)


def trade(axis, source, target, send, recv):
    w, n = lax.axis_index("wide"), lax.axis_index("narrow")
    peers = source.shape[0]
    here = w if axis == "wide" else n
    copies = []
    for d in range(1, peers):
        to = lax.rem(here + d, peers)
        copies.append(
            pltpu.make_async_remote_copy(
                src_ref=source.at[to],
                dst_ref=target.at[here],
                send_sem=send.at[d],
                recv_sem=recv.at[d],
                device_id=(to, n) if axis == "wide" else (w, to),
                device_id_type=MESH,
            )
        )
    for copy in copies:
        copy.start()
    target[here] = source[here]
    for copy in copies:
        copy.wait()


def turn(source, target):
    outer = source.shape[0]
    inner = target.shape[0]
    count = source.shape[1] // inner
    for a in range(outer):
        for b in range(inner):
            target[b, a * count : (a + 1) * count, :] = source[a, b * count : (b + 1) * count, :]


def exact(a, b):
    return jnp.dot(a, b, precision=HIGHEST, preferred_element_type=jnp.float32)


def close(a, b):
    a_high, a_low = split(a)
    b_high, b_low = split(b)
    return dot(a_high, b_high) + dot(a_low, b_high) + dot(a_high, b_low)


def interfaces(traces, t, gain, decay, modes_ref, place, jumps, fluxes, wide, narrow):
    total = traces.shape[0]
    count = total // (wide * narrow)
    span = narrow * count
    rows, lines = t["box_modes"].shape
    row = lax.broadcasted_iota(jnp.int32, (total, 1), 0)
    has_wide = row >= span
    has_narrow = (row & (span - 1)) >= count
    own_mode = row & (count - 1)
    holds_steady = place == 0

    def up(x, by):
        return pltpu.roll(x, total - by, 0)

    def by_mode(x, weights):
        out = close(x, weights[0])
        for mode in range(1, count):
            out = jnp.where(own_mode == mode, close(x, weights[mode]), out)
        return out

    def influence(box_modes, faces, side, first):
        weights = []
        low = lax.broadcasted_iota(jnp.int32, box_modes.shape, 0) == 0
        left = lax.broadcasted_iota(jnp.int32, box_modes.shape, 1) == 0
        for mode in range(count):
            shift = modes_ref[place * count + mode]
            eig = box_modes[...] + shift
            some = eig > 0.0
            value = jnp.where(some, faces[side] / eig, faces[side] if first else 0.0)
            if first and mode == 0:
                value = jnp.where(low & jnp.logical_not(left) & holds_steady, 0.0, value)
            weights.append(value)
        return weights

    alternate = t["alternate"][:1, :]
    wide_low, wide_high = traces[:, :lines], traces[:, LANES : LANES + lines]
    narrow_low, narrow_high = traces[:, 2 * LANES : 2 * LANES + rows], traces[:, 2 * LANES + rows : 2 * LANES + 2 * rows]
    jump_narrow = jnp.where(has_narrow, narrow_low - pltpu.roll(narrow_high, count, 0), 0.0)
    jump_wide = jnp.where(has_wide, wide_low - pltpu.roll(wide_high, span, 0), 0.0)
    gain = jnp.concatenate([gain[:, :rows]] * wide, axis=0)
    sine = t["sine"][...]

    def glued(jump):
        return close(sine, gain * close(sine, jump))

    row_zero = lax.broadcasted_iota(jnp.int32, (total, rows), 1) == 0
    flux = glued(jump_narrow)
    steady = close(t["steady"][...], jump_narrow)
    flux = flux + jnp.where(row_zero & holds_steady, steady, 0.0)
    moved = []
    for side in range(2):
        value = by_mode(flux, influence(t["box_modes"], t["faces"], side, True))
        moved.append(alternate[:, :lines] * up(value, count) - value)
    jump_wide = jump_wide + jnp.where(has_wide, moved[0] - pltpu.roll(moved[1], span, 0), 0.0)
    pad = jnp.zeros((total, LANES - lines), jnp.float32)
    jumps[...] = jnp.concatenate([jump_wide, pad], axis=1)
    joined = jnp.zeros((count * wide, lines * narrow), jnp.float32)
    for J in range(narrow):
        part = [jumps[pl.ds(J * count + mode, wide, stride=span), :] for mode in range(count)]
        joined = joined + from_right(
            jnp.concatenate(part, axis=0)[:, :lines], t["join_high"][J], t["join_low"][J]
        )
    wide_gain = []
    for mode in range(count):
        at, top = decay[2 * mode : 2 * mode + 1], decay[2 * mode + 1 : 2 * mode + 2]
        wide_gain.append(top / (at * at + 2.0 * (1.0 + at) * t["angle"][...]))
    wide_sine = t["wide_sine"][...]
    shaped = close(wide_sine, jnp.concatenate(wide_gain, axis=0) * close(wide_sine, joined))
    pad = jnp.zeros((wide, LANES - lines), jnp.float32)
    for J in range(narrow):
        part = from_right(shaped, t["part_high"][J], t["part_low"][J])
        for mode in range(count):
            fluxes[pl.ds(J * count + mode, wide, stride=span), :] = jnp.concatenate(
                [part[mode * wide : (mode + 1) * wide], pad], axis=1
            )
    padded_wide = fluxes[...]
    flux_wide = padded_wide[:, :lines]
    moved = []
    for side in range(2):
        value = by_mode(flux_wide, influence(t["box_modes_turned"], t["faces_turned"], side, False))
        moved.append(alternate[:, :rows] * up(value, span) - value)
    jump_narrow = jump_narrow + jnp.where(has_narrow, moved[0] - pltpu.roll(moved[1], count, 0), 0.0)
    flux_narrow = glued(jump_narrow)
    padded_high = up(padded_wide, span)
    balanced = exact(t["balance"][...], (padded_high - padded_wide)[:, :rows])
    level = exact(t["level_flux"][...], balanced) + exact(t["level_jump"][...], jump_narrow)
    level = level + exact(t["level_wide"][...], joined[:, :rows])
    flux_narrow = jnp.where(row_zero & (own_mode == 0) & holds_steady, balanced, flux_narrow)
    rest = level[:, : LANES - 2 * rows]
    return jnp.concatenate([padded_wide, padded_high, flux_narrow, up(flux_narrow, count), rest], axis=1)


def forward_exchange_kernel(steps, groups, wide, narrow, *refs):
    step = pl.program_id(0)
    names = len(FIXED)
    box_in, refs = refs[:11], refs[11:]
    sources, gain_hbm, decay_hbm, modes_ref = refs[:names], refs[names], refs[names + 1], refs[names + 2]
    spectrum_ref, wide_ref, narrow_ref, level_ref = refs[names + 3 : names + 7]
    refs = refs[names + 7 :]
    carry, held, wide_face, narrow_face, wide_in, narrow_in = refs[:6]
    fixed, refs = refs[6 : 6 + names], refs[6 + names :]
    gain, decay, near_a, near_b, far_a, far_b, near_c, far_c, jumps, fluxes = refs[:10]
    table_sem, near_send, near_recv, far_send, far_recv, near_send2, near_recv2, far_send2, far_recv2 = refs[10:]
    lines, depth = wide_in.shape[1:]
    rows = narrow_in.shape[1]
    count = depth // (wide * narrow)
    place = lax.axis_index("narrow") * wide + lax.axis_index("wide")
    per_block = 8 // (2 * count)
    own = [(gain_hbm.at[place], gain), (decay_hbm.at[lax.div(place, per_block)], decay)]
    pairs = list(zip(sources, fixed)) + own

    @pl.when(step == 0)
    def _():
        greet(wide, narrow)
        for copy in prepared(pairs, table_sem):
            copy.start()

    forward_kernel(steps, *box_in, spectrum_ref, wide_in, narrow_in, carry, held, wide_face, narrow_face)

    @pl.when(step == steps + groups - 1)
    def _():
        gap = jnp.zeros((LANES - lines, depth), jnp.float32)
        rest = jnp.zeros((LANES - 2 * rows, depth), jnp.float32)
        values = jnp.concatenate([wide_in[0], gap, wide_in[1], gap, narrow_in[0], narrow_in[1], rest], axis=0).T
        far_rows = wide * count
        for p in range(narrow):
            near_a[p] = values[p * far_rows : (p + 1) * far_rows]
        pl.semaphore_wait(pltpu.get_barrier_semaphore(), wide + narrow - 2)
        trade("narrow", near_a, near_b, near_send, near_recv)
        turn(near_b, far_a)
        trade("wide", far_a, far_b, far_send, far_recv)
        for copy in prepared(pairs, table_sem):
            copy.wait()
        traces = jnp.concatenate([far_b[p] for p in range(wide)], axis=0)
        here = lax.rem(place, per_block)
        own_decay = decay[: 2 * count]
        for p in range(1, per_block):
            own_decay = jnp.where(here == p, decay[p * 2 * count : (p + 1) * 2 * count], own_decay)
        table = dict(zip(FIXED, fixed))
        out = interfaces(traces, table, gain[...], own_decay, modes_ref, place, jumps, fluxes, wide, narrow)
        span = narrow * count
        for p in range(wide):
            far_a[p] = out[p * span : (p + 1) * span]
        trade("wide", far_a, far_c, far_send2, far_recv2)
        turn(far_c, near_a)
        trade("narrow", near_a, near_c, near_send2, near_recv2)
        values = jnp.concatenate([near_c[p] for p in range(narrow)], axis=0).T
        wide_ref[0] = values[:lines]
        wide_ref[1] = values[LANES : LANES + lines]
        narrow_ref[0] = values[2 * LANES : 2 * LANES + rows]
        narrow_ref[1] = values[2 * LANES + rows : 2 * LANES + 2 * rows]
        level_ref[...] = values[2 * (LANES + rows) : 2 * (LANES + rows) + 8]


def prepared(pairs, sem):
    return [pltpu.make_async_copy(source, target, sem.at[i]) for i, (source, target) in enumerate(pairs)]


IN_VMEM = pl.BlockSpec(memory_space=pltpu.VMEM)
IN_HBM = pl.BlockSpec(memory_space=pl.ANY)
IN_SMEM = pl.BlockSpec(memory_space=pltpu.SMEM)


VMEM_LIMIT = 60 * 2**20
BLOCK = 16
GROUP = 16


def box_tables(rows, lines, depth):
    shift = modes(rows)[:, None] + modes(depth)[None, :]
    low = np.broadcast_to(face(rows)[:, None], (rows, depth))
    high = np.broadcast_to((face(rows) * signs(rows))[:, None], (rows, depth))
    faces = np.stack([low, high])
    return [jnp.asarray(v, jnp.float32) for v in (shift, faces, modes(lines), face(lines))]


def whole(*shape):
    return pl.BlockSpec(shape, lambda s: (0,) * len(shape))


def table_specs(rows, lines, depth):
    return [
        whole(depth, depth),
        whole(depth, depth),
        whole(2 * lines, 2 * lines),
        whole(2 * rows, 2 * rows),
        whole(rows, depth),
        whole(2, rows, depth),
        pl.BlockSpec(memory_space=pltpu.SMEM),
        pl.BlockSpec(memory_space=pltpu.SMEM),
    ]


def forward_exchange(first, second, third, wide, narrow):
    rows, lines, depth = first.shape
    steps, groups = rows // BLOCK, lines // GROUP
    count = depth // (wide * narrow)
    slab = pl.BlockSpec((BLOCK, lines, depth), lambda s: (jnp.minimum(s, steps - 1), 0, 0))
    depth_high, depth_low = halves(cosine_matrix(depth).T)
    t = tables(rows, lines, depth, wide, narrow)
    width = 3 * LANES
    near = (narrow, wide * count, width)
    far = (wide, narrow * count, width)
    face_rows = (wide * narrow * count, LANES)
    f32 = jnp.float32
    fixed = [jnp.asarray(t[name]) for name in FIXED]
    box_shapes = [
        (lines, depth),
        (depth // LANES, rows * lines, LANES),
        (lines, depth),
        (rows, depth),
        (2, lines, depth),
        (2, rows, depth),
    ]
    shapes = [t["gain"].shape[1:], t["decay"].shape[1:], near, near, far, far, near, far, face_rows, face_rows]
    sems = [len(fixed) + 2, narrow, narrow, wide, wide, narrow, narrow, wide, wide]
    return pl.pallas_call(
        functools.partial(forward_exchange_kernel, steps, groups, wide, narrow),
        grid=(steps + groups,),
        out_shape=[
            jax.ShapeDtypeStruct((lines, rows, depth), f32),
            jax.ShapeDtypeStruct((2, lines, depth), f32),
            jax.ShapeDtypeStruct((2, rows, depth), f32),
            jax.ShapeDtypeStruct((8, depth), f32),
        ],
        in_specs=[slab, slab, slab]
        + table_specs(rows, lines, depth)
        + [IN_HBM] * (len(fixed) + 2)
        + [IN_SMEM],
        out_specs=[
            pl.BlockSpec((GROUP, rows, depth), lambda s: (jnp.maximum(s - steps, 0), 0, 0)),
            whole(2, lines, depth),
            whole(2, rows, depth),
            whole(8, depth),
        ],
        scratch_shapes=[pltpu.VMEM(v, f32) for v in box_shapes]
        + [pltpu.VMEM(v.shape, v.dtype) for v in fixed]
        + [pltpu.VMEM(v, f32) for v in shapes]
        + [pltpu.SemaphoreType.DMA((k,)) for k in sems],
        compiler_params=pltpu.CompilerParams(
            collective_id=0, has_side_effects=True, vmem_limit_bytes=VMEM_LIMIT
        ),
    )(
        first,
        second,
        third,
        jnp.asarray(depth_high),
        jnp.asarray(depth_low),
        jnp.asarray(left_table(cosine_matrix(lines))),
        jnp.asarray(left_table(cosine_matrix(rows))),
        *box_tables(rows, lines, depth),
        *fixed,
        jnp.asarray(t["gain"]),
        jnp.asarray(t["decay"]),
        jnp.asarray(modes(depth), f32),
    )


def inverse(spectrum, wide_flux, narrow_flux, level):
    lines, rows, depth = spectrum.shape
    steps, groups = rows // BLOCK, lines // GROUP
    depth_high, depth_low = halves(cosine_matrix(depth))
    return pl.pallas_call(
        functools.partial(inverse_kernel, groups),
        grid=(steps + groups,),
        out_shape=jax.ShapeDtypeStruct((rows, lines, depth), jnp.float32),
        in_specs=[
            pl.BlockSpec((GROUP, rows, depth), lambda s: (jnp.minimum(s, groups - 1), 0, 0)),
            pl.BlockSpec((2, GROUP, depth), lambda s: (0, jnp.minimum(s, groups - 1), 0)),
            whole(2, rows, depth),
            whole(8, depth),
        ]
        + table_specs(rows, lines, depth),
        out_specs=pl.BlockSpec((BLOCK, lines, depth), lambda s: (jnp.maximum(s - groups, 0), 0, 0)),
        scratch_shapes=[pltpu.VMEM((depth // LANES, rows * lines, LANES), jnp.float32)],
        compiler_params=pltpu.CompilerParams(vmem_limit_bytes=VMEM_LIMIT),
    )(
        spectrum,
        wide_flux,
        narrow_flux,
        level,
        jnp.asarray(depth_high),
        jnp.asarray(depth_low),
        jnp.asarray(left_table(cosine_matrix(lines).T)),
        jnp.asarray(left_table(cosine_matrix(rows).T)),
        *box_tables(rows, lines, depth),
    )


def shards(slope_first, slope_second, slope_third):
    rows, lines, depth = slope_first.shape
    wide = lax.axis_size("wide")
    narrow = lax.axis_size("narrow")
    spectrum, wide_flux, narrow_flux, level = forward_exchange(slope_first, slope_second, slope_third, wide, narrow)
    return inverse(spectrum, wide_flux, narrow_flux, level)


def solution(mesh):
    placed = P("wide", "narrow", None)
    return jax.shard_map(shards, mesh=mesh, in_specs=(placed, placed, placed), out_specs=placed, check_vma=False)
```

```python
import functools
import math

import jax
import jax.numpy as jnp
import numpy as np
from jax import lax
from jax.experimental import pallas as pl
from jax.experimental.pallas import tpu as pltpu
from jax.sharding import PartitionSpec as P


LANES = 128


def cosine_matrix(length):
    k = np.arange(length)[:, None]
    n = np.arange(length)[None, :]
    table = np.sqrt(2.0 / length) * np.cos(np.pi * ((2 * n + 1) * k % (4 * length)) / (2 * length))
    table[0] = np.sqrt(1.0 / length)
    return table


def sine_matrix(parts):
    m = np.arange(1, parts)
    return np.sqrt(2.0 / parts) * np.sin(np.pi * m[:, None] * m[None, :] / parts)


def modes(length):
    return 4.0 * np.sin(np.pi * np.arange(length) / (2 * length)) ** 2


def signs(length):
    return (-1.0) ** np.arange(length)


def face(length):
    return cosine_matrix(length)[:, 0]


def exponent(mu):
    return 2.0 * np.arcsinh(np.sqrt(mu) / 2.0)


def interface_gain(mu, cells, parts):
    kappa = exponent(mu)[..., None]
    angle = np.pi * np.arange(1, parts) / parts
    decay = np.exp(-kappa * cells)
    ratio = -np.expm1(-2.0 * kappa * cells) / (np.expm1(-kappa * cells) ** 2 + 2.0 * decay * (1.0 - np.cos(angle)))
    return np.tanh(kappa / 2.0) * ratio


def running_levels(parts):
    part = np.arange(parts)[:, None]
    step = np.arange(1, parts)[None, :]
    return (step <= part) - (parts - step) / parts


def bordered(matrix, top, left):
    return np.pad(matrix, ((top, 0), (left, 0)))


def lane_padded(table):
    pad = [(0, 0)] * (table.ndim - 1) + [(0, -table.shape[-1] % LANES)]
    return np.pad(table, pad)


@functools.lru_cache(None)
def tables(rows, lines, depth, wide, narrow):
    count = depth // (wide * narrow)
    row_modes, line_modes, depth_modes = modes(rows), modes(lines), modes(depth)
    row_face, line_face = face(rows), face(lines)
    own_all = np.eye(count)
    own_first = np.zeros((count, count))
    own_first[0, 0] = 1.0

    def over_narrow(matrix, own):
        return np.kron(np.eye(wide), np.kron(matrix, own))

    t = {}
    t["sine"] = over_narrow(bordered(sine_matrix(narrow), 1, 1), own_all)
    levels = running_levels(narrow)
    steady = np.cumsum(-levels / line_face[0], axis=0)[:-1] / line_face[0]
    t["steady"] = over_narrow(bordered(steady, 1, 1), own_first)
    balance = -(row_face[0] / line_face[0]) * np.tril(np.ones((narrow - 1, narrow)))
    t["balance"] = over_narrow(bordered(balance, 1, 0), own_first)
    k = np.arange(1, lines)
    near = np.sum(line_face[k] ** 2 / line_modes[k])
    far = np.sum(signs(lines)[k] * line_face[k] ** 2 / line_modes[k])
    link = (1.0 + 2.0 * near) * np.eye(narrow - 1) - far * (np.eye(narrow - 1, k=1) + np.eye(narrow - 1, k=-1))
    t["level_flux"] = over_narrow(bordered(levels @ link / line_face[0], 0, 1), own_first)
    t["level_jump"] = over_narrow(bordered(-levels / line_face[0], 0, 1), own_first)
    level_wide = bordered(-running_levels(wide) / (row_face[0] * math.sqrt(narrow)), 0, 1)
    first_column = np.zeros((count, 1))
    first_column[0, 0] = 1.0
    t["level_wide"] = np.kron(first_column.T, np.kron(level_wide, np.kron(np.ones((narrow, 1)), first_column)))
    gain = interface_gain(depth_modes[:, None] + row_modes[None, :], lines, narrow)
    gain[0, 0, :] = 0.0
    gain = bordered(np.moveaxis(gain, 2, 1).reshape(depth * (narrow - 1), rows), 0, 0)
    gain = np.pad(gain.reshape(depth, narrow - 1, rows), ((0, 0), (1, 0), (0, 0)))
    gain = gain.reshape(wide * narrow, count, narrow, rows).swapaxes(1, 2)
    t["gain"] = lane_padded(gain.reshape(wide * narrow, narrow * count, rows))
    full = cosine_matrix(lines * narrow).reshape(lines * narrow, narrow, lines)
    join = np.einsum("qJn,kn->Jkq", full, cosine_matrix(lines))
    t["join_high"], t["join_low"] = halves(join)
    t["part_high"], t["part_low"] = halves(np.swapaxes(join, 1, 2))
    shift = depth_modes[:, None] + modes(lines * narrow)[None, :]
    decay = np.expm1(-exponent(shift) * rows)
    top = -np.sqrt(shift / (4.0 + shift)) * decay * (2.0 + decay)
    t["decay"] = np.stack([decay, top], axis=1).reshape(-1, 8, lines * narrow)
    t["wide_sine"] = np.kron(own_all, bordered(sine_matrix(wide), 1, 1))
    angle = 1.0 - np.cos(np.pi * np.arange(wide) / wide)
    angle[0] = 1.0
    t["angle"] = np.broadcast_to(angle[:, None], (wide, lines * narrow))
    t["box_modes"] = row_modes[:, None] + line_modes[None, :]
    both = row_face[:, None] * line_face[None, :]
    t["faces"] = np.stack([both, both * signs(rows)[:, None]])
    t["box_modes_turned"] = t["box_modes"].T
    t["faces_turned"] = np.stack([both.T, both.T * signs(lines)[:, None]])
    t["alternate"] = np.broadcast_to(signs(LANES)[None, :], (8, LANES))
    return {
        name: np.ascontiguousarray(value, dtype=jnp.bfloat16 if name[:4] in ("join", "part") else np.float32)
        for name, value in t.items()
    }


FIXED = (
    "sine",
    "steady",
    "balance",
    "level_flux",
    "level_jump",
    "level_wide",
    "join_high",
    "join_low",
    "part_high",
    "part_low",
    "wide_sine",
    "angle",
    "box_modes",
    "faces",
    "box_modes_turned",
    "faces_turned",
    "alternate",
)


def halves(table):
    table = np.asarray(table, np.float32)
    high = table.astype(jnp.bfloat16)
    low = (table - high.astype(np.float32)).astype(jnp.bfloat16)
    return high, low


def left_table(table):
    high, low = halves(table)
    return np.block([[high, high], [low, np.zeros_like(low)]])


def split(x):
    high = x.astype(jnp.bfloat16)
    return high, (x - high.astype(jnp.float32)).astype(jnp.bfloat16)


def dot(a, b):
    return jnp.dot(a, b, preferred_element_type=jnp.float32)


def from_left(table, x):
    both = dot(table, jnp.concatenate(split(x), axis=0))
    count = x.shape[0]
    return both[:count] + both[count:]


def from_right(x, high_table, low_table):
    high, low = split(x)
    return dot(high, high_table) + dot(low, high_table) + dot(high, low_table)


def lower_neighbour(x, axis):
    index = lax.broadcasted_iota(jnp.int32, x.shape, axis)
    x = jnp.where(index < x.shape[axis] - 1, x, 0.0)
    return pltpu.roll(x, 1, axis) - x


def put(held, where, value):
    for panel in range(held.shape[0]):
        held[panel, where, :] = value[:, panel * LANES : (panel + 1) * LANES]


def take(held, where):
    return jnp.concatenate([held[panel, where, :] for panel in range(held.shape[0])], axis=1)


def forward_kernel(
    steps,
    first_ref,
    second_ref,
    third_ref,
    depth_high_ref,
    depth_low_ref,
    line_ref,
    row_ref,
    shift_ref,
    faces_ref,
    line_shift_ref,
    line_face_ref,
    out_ref,
    wide_ref,
    narrow_ref,
    carry,
    held,
    wide_face,
    narrow_face,
):
    step = pl.program_id(0)
    rows, lines = row_ref.shape[0] // 2, line_ref.shape[0] // 2
    block = first_ref.shape[0]
    group = out_ref.shape[0]

    @pl.when(step == 0)
    def _():
        carry[...] = jnp.zeros_like(carry)

    @pl.when(step < steps)
    def _():
        below = carry[...]
        parts = []
        for i in range(block):
            here = first_ref[i]
            if i == block - 1:
                here = jnp.where(step < steps - 1, here, 0.0)
            part = below - here + lower_neighbour(second_ref[i], 0) + lower_neighbour(third_ref[i], 1)
            below = here
            parts.append(part)
            narrow_face[pl.ds(step * block + i, 1), :] = second_ref[i, lines - 1 : lines, :]
        carry[...] = below
        stacked = from_right(jnp.concatenate(parts, axis=0), depth_high_ref[...], depth_low_ref[...])
        for i in range(block):
            part = from_left(line_ref[...], stacked[i * lines : (i + 1) * lines])
            put(held, pl.ds(pl.multiple_of((step * block + i) * lines, 8), lines), part)

    @pl.when(step == steps)
    def _():
        face = from_right(first_ref[block - 1], depth_high_ref[...], depth_low_ref[...])
        wide_face[...] = from_left(line_ref[...], face)
        face = from_right(narrow_face[...], depth_high_ref[...], depth_low_ref[...])
        narrow_ref[0] = jnp.zeros_like(face)
        narrow_ref[1] = from_left(row_ref[...], face)

    @pl.when(step >= steps)
    def _():
        lows, highs = [], []
        narrow_low, narrow_high = narrow_ref[0], narrow_ref[1]
        for i in range(group):
            line = (step - steps) * group + i
            part = from_left(row_ref[...], take(held, pl.ds(line, rows, stride=lines)))
            out_ref[i] = part
            eig = shift_ref[...] + line_shift_ref[line]
            closed = jnp.where(eig > 0.0, part / eig, 0.0)
            lows.append(jnp.sum(closed * faces_ref[0], axis=0, keepdims=True))
            highs.append(jnp.sum(closed * faces_ref[1], axis=0, keepdims=True))
            closed = closed * line_face_ref[line]
            narrow_low = narrow_low + closed
            narrow_high = narrow_high + closed if i % 2 == 0 else narrow_high - closed
        here = pl.ds(pl.multiple_of((step - steps) * group, 8), group)
        wide_ref[0, here, :] = jnp.concatenate(lows, axis=0)
        wide_ref[1, here, :] = jnp.concatenate(highs, axis=0) + wide_face[here, :]
        narrow_ref[0] = narrow_low
        narrow_ref[1] = narrow_high


def inverse_kernel(
    steps,
    spectrum_ref,
    wide_ref,
    narrow_ref,
    level_ref,
    depth_high_ref,
    depth_low_ref,
    line_ref,
    row_ref,
    shift_ref,
    faces_ref,
    line_shift_ref,
    line_face_ref,
    out_ref,
    held,
):
    step = pl.program_id(0)
    rows, lines = row_ref.shape[0] // 2, line_ref.shape[0] // 2
    block = out_ref.shape[0]
    group = spectrum_ref.shape[0]

    @pl.when(step < steps)
    def _():
        for i in range(group):
            line = step * group + i
            added = faces_ref[1] * wide_ref[1, i : i + 1, :] - faces_ref[0] * wide_ref[0, i : i + 1, :]
            turned = narrow_ref[1] if i % 2 == 0 else -narrow_ref[1]
            part = spectrum_ref[i] + added + line_face_ref[line] * (turned - narrow_ref[0])
            eig = shift_ref[...] + line_shift_ref[line]
            part = jnp.where(eig > 0.0, part / eig, level_ref[:1])
            put(held, pl.ds(line, rows, stride=lines), from_left(row_ref[...], part))

    @pl.when(step >= steps)
    def _():
        parts = []
        for i in range(block):
            here = pl.multiple_of(((step - steps) * block + i) * lines, 8)
            parts.append(from_left(line_ref[...], take(held, pl.ds(here, lines))))
        result = from_right(jnp.concatenate(parts, axis=0), depth_high_ref[...], depth_low_ref[...])
        for i in range(block):
            out_ref[i] = result[i * lines : (i + 1) * lines]


MESH = pl.DeviceIdType.MESH


def greet(wide, narrow):
    w, n = lax.axis_index("wide"), lax.axis_index("narrow")
    barrier = pltpu.get_barrier_semaphore()
    for d in range(1, narrow):
        pl.semaphore_signal(barrier, inc=1, device_id=(w, lax.rem(n + d, narrow)), device_id_type=MESH)
    for d in range(1, wide):
        pl.semaphore_signal(barrier, inc=1, device_id=(lax.rem(w + d, wide), n), device_id_type=MESH)


def trade(axis, source, target, send, recv):
    w, n = lax.axis_index("wide"), lax.axis_index("narrow")
    peers = source.shape[0]
    here = w if axis == "wide" else n
    copies = []
    for d in range(1, peers):
        to = lax.rem(here + d, peers)
        copies.append(
            pltpu.make_async_remote_copy(
                src_ref=source.at[to],
                dst_ref=target.at[here],
                send_sem=send.at[d],
                recv_sem=recv.at[d],
                device_id=(to, n) if axis == "wide" else (w, to),
                device_id_type=MESH,
            )
        )
    for copy in copies:
        copy.start()
    target[here] = source[here]
    for copy in copies:
        copy.wait()


def turn(source, target):
    outer = source.shape[0]
    inner = target.shape[0]
    count = source.shape[1] // inner
    for a in range(outer):
        for b in range(inner):
            target[b, a * count : (a + 1) * count, :] = source[a, b * count : (b + 1) * count, :]


def close(a, b):
    a_high, a_low = split(a)
    b_high, b_low = split(b)
    return dot(a_high, b_high) + dot(a_low, b_high) + dot(a_high, b_low)


def interfaces(traces, t, gain, decay, modes_ref, place, jumps, fluxes, wide, narrow):
    total = traces.shape[0]
    count = total // (wide * narrow)
    span = narrow * count
    rows, lines = t["box_modes"].shape
    row = lax.broadcasted_iota(jnp.int32, (total, 1), 0)
    has_wide = row >= span
    has_narrow = (row & (span - 1)) >= count
    own_mode = row & (count - 1)
    holds_steady = place == 0

    def up(x, by):
        return pltpu.roll(x, total - by, 0)

    def by_mode(x, weights):
        out = close(x, weights[0])
        for mode in range(1, count):
            out = jnp.where(own_mode == mode, close(x, weights[mode]), out)
        return out

    def influence(box_modes, faces, side, first):
        weights = []
        low = lax.broadcasted_iota(jnp.int32, box_modes.shape, 0) == 0
        left = lax.broadcasted_iota(jnp.int32, box_modes.shape, 1) == 0
        for mode in range(count):
            shift = modes_ref[place * count + mode]
            eig = box_modes[...] + shift
            some = eig > 0.0
            value = jnp.where(some, faces[side] / eig, faces[side] if first else 0.0)
            if first and mode == 0:
                value = jnp.where(low & jnp.logical_not(left) & holds_steady, 0.0, value)
            weights.append(value)
        return weights

    alternate = t["alternate"][:1, :]
    wide_low, wide_high = traces[:, :lines], traces[:, LANES : LANES + lines]
    narrow_low, narrow_high = traces[:, 2 * LANES : 2 * LANES + rows], traces[:, 2 * LANES + rows : 2 * LANES + 2 * rows]
    jump_narrow = jnp.where(has_narrow, narrow_low - pltpu.roll(narrow_high, count, 0), 0.0)
    jump_wide = jnp.where(has_wide, wide_low - pltpu.roll(wide_high, span, 0), 0.0)
    gain = jnp.concatenate([gain[:, :rows]] * wide, axis=0)
    sine = t["sine"][...]

    def glued(jump):
        return close(sine, gain * close(sine, jump))

    row_zero = lax.broadcasted_iota(jnp.int32, (total, rows), 1) == 0
    flux = glued(jump_narrow)
    steady = close(t["steady"][...], jump_narrow)
    flux = flux + jnp.where(row_zero & holds_steady, steady, 0.0)
    moved = []
    for side in range(2):
        value = by_mode(flux, influence(t["box_modes"], t["faces"], side, True))
        moved.append(alternate[:, :lines] * up(value, count) - value)
    jump_wide = jump_wide + jnp.where(has_wide, moved[0] - pltpu.roll(moved[1], span, 0), 0.0)
    pad = jnp.zeros((total, LANES - lines), jnp.float32)
    jumps[...] = jnp.concatenate([jump_wide, pad], axis=1)
    joined = jnp.zeros((count * wide, lines * narrow), jnp.float32)
    for J in range(narrow):
        part = [jumps[pl.ds(J * count + mode, wide, stride=span), :] for mode in range(count)]
        joined = joined + from_right(
            jnp.concatenate(part, axis=0)[:, :lines], t["join_high"][J], t["join_low"][J]
        )
    wide_gain = []
    for mode in range(count):
        at, top = decay[2 * mode : 2 * mode + 1], decay[2 * mode + 1 : 2 * mode + 2]
        wide_gain.append(top / (at * at + 2.0 * (1.0 + at) * t["angle"][...]))
    wide_sine = t["wide_sine"][...]
    shaped = close(wide_sine, jnp.concatenate(wide_gain, axis=0) * close(wide_sine, joined))
    pad = jnp.zeros((wide, LANES - lines), jnp.float32)
    for J in range(narrow):
        part = from_right(shaped, t["part_high"][J], t["part_low"][J])
        for mode in range(count):
            fluxes[pl.ds(J * count + mode, wide, stride=span), :] = jnp.concatenate(
                [part[mode * wide : (mode + 1) * wide], pad], axis=1
            )
    padded_wide = fluxes[...]
    flux_wide = padded_wide[:, :lines]
    moved = []
    for side in range(2):
        value = by_mode(flux_wide, influence(t["box_modes_turned"], t["faces_turned"], side, False))
        moved.append(alternate[:, :rows] * up(value, span) - value)
    jump_narrow = jump_narrow + jnp.where(has_narrow, moved[0] - pltpu.roll(moved[1], count, 0), 0.0)
    flux_narrow = glued(jump_narrow)
    padded_high = up(padded_wide, span)
    balanced = close(t["balance"][...], (padded_high - padded_wide)[:, :rows])
    level = close(t["level_flux"][...], balanced) + close(t["level_jump"][...], jump_narrow)
    level = level + close(t["level_wide"][...], joined[:, :rows])
    flux_narrow = jnp.where(row_zero & (own_mode == 0) & holds_steady, balanced, flux_narrow)
    rest = level[:, : LANES - 2 * rows]
    return jnp.concatenate([padded_wide, padded_high, flux_narrow, up(flux_narrow, count), rest], axis=1)


def forward_exchange_kernel(steps, groups, wide, narrow, *refs):
    step = pl.program_id(0)
    names = len(FIXED)
    box_in, refs = refs[:11], refs[11:]
    sources, gain_hbm, decay_hbm, modes_ref = refs[:names], refs[names], refs[names + 1], refs[names + 2]
    spectrum_ref, wide_ref, narrow_ref, level_ref = refs[names + 3 : names + 7]
    refs = refs[names + 7 :]
    carry, held, wide_face, narrow_face, wide_in, narrow_in = refs[:6]
    fixed, refs = refs[6 : 6 + names], refs[6 + names :]
    gain, decay, near_a, near_b, far_a, far_b, near_c, far_c, jumps, fluxes = refs[:10]
    table_sem, near_send, near_recv, far_send, far_recv, near_send2, near_recv2, far_send2, far_recv2 = refs[10:]
    lines, depth = wide_in.shape[1:]
    rows = narrow_in.shape[1]
    count = depth // (wide * narrow)
    place = lax.axis_index("narrow") * wide + lax.axis_index("wide")
    per_block = 8 // (2 * count)
    own = [(gain_hbm.at[place], gain), (decay_hbm.at[lax.div(place, per_block)], decay)]
    pairs = list(zip(sources, fixed)) + own

    @pl.when(step == 0)
    def _():
        greet(wide, narrow)
        for copy in prepared(pairs, table_sem):
            copy.start()

    forward_kernel(steps, *box_in, spectrum_ref, wide_in, narrow_in, carry, held, wide_face, narrow_face)

    @pl.when(step == steps + groups - 1)
    def _():
        gap = jnp.zeros((LANES - lines, depth), jnp.float32)
        rest = jnp.zeros((LANES - 2 * rows, depth), jnp.float32)
        values = jnp.concatenate([wide_in[0], gap, wide_in[1], gap, narrow_in[0], narrow_in[1], rest], axis=0).T
        far_rows = wide * count
        for p in range(narrow):
            near_a[p] = values[p * far_rows : (p + 1) * far_rows]
        pl.semaphore_wait(pltpu.get_barrier_semaphore(), wide + narrow - 2)
        trade("narrow", near_a, near_b, near_send, near_recv)
        turn(near_b, far_a)
        trade("wide", far_a, far_b, far_send, far_recv)
        for copy in prepared(pairs, table_sem):
            copy.wait()
        traces = jnp.concatenate([far_b[p] for p in range(wide)], axis=0)
        here = lax.rem(place, per_block)
        own_decay = decay[: 2 * count]
        for p in range(1, per_block):
            own_decay = jnp.where(here == p, decay[p * 2 * count : (p + 1) * 2 * count], own_decay)
        table = dict(zip(FIXED, fixed))
        out = interfaces(traces, table, gain[...], own_decay, modes_ref, place, jumps, fluxes, wide, narrow)
        span = narrow * count
        for p in range(wide):
            far_a[p] = out[p * span : (p + 1) * span]
        trade("wide", far_a, far_c, far_send2, far_recv2)
        turn(far_c, near_a)
        trade("narrow", near_a, near_c, near_send2, near_recv2)
        values = jnp.concatenate([near_c[p] for p in range(narrow)], axis=0).T
        wide_ref[0] = values[:lines]
        wide_ref[1] = values[LANES : LANES + lines]
        narrow_ref[0] = values[2 * LANES : 2 * LANES + rows]
        narrow_ref[1] = values[2 * LANES + rows : 2 * LANES + 2 * rows]
        level_ref[...] = values[2 * (LANES + rows) : 2 * (LANES + rows) + 8]


def prepared(pairs, sem):
    return [pltpu.make_async_copy(source, target, sem.at[i]) for i, (source, target) in enumerate(pairs)]


IN_VMEM = pl.BlockSpec(memory_space=pltpu.VMEM)
IN_HBM = pl.BlockSpec(memory_space=pl.ANY)
IN_SMEM = pl.BlockSpec(memory_space=pltpu.SMEM)


VMEM_LIMIT = 60 * 2**20
BLOCK = 16
GROUP = 16


def box_tables(rows, lines, depth):
    shift = modes(rows)[:, None] + modes(depth)[None, :]
    low = np.broadcast_to(face(rows)[:, None], (rows, depth))
    high = np.broadcast_to((face(rows) * signs(rows))[:, None], (rows, depth))
    faces = np.stack([low, high])
    return [jnp.asarray(v, jnp.float32) for v in (shift, faces, modes(lines), face(lines))]


def whole(*shape):
    return pl.BlockSpec(shape, lambda s: (0,) * len(shape))


def table_specs(rows, lines, depth):
    return [
        whole(depth, depth),
        whole(depth, depth),
        whole(2 * lines, 2 * lines),
        whole(2 * rows, 2 * rows),
        whole(rows, depth),
        whole(2, rows, depth),
        pl.BlockSpec(memory_space=pltpu.SMEM),
        pl.BlockSpec(memory_space=pltpu.SMEM),
    ]


def forward_exchange(first, second, third, wide, narrow):
    rows, lines, depth = first.shape
    steps, groups = rows // BLOCK, lines // GROUP
    count = depth // (wide * narrow)
    slab = pl.BlockSpec((BLOCK, lines, depth), lambda s: (jnp.minimum(s, steps - 1), 0, 0))
    depth_high, depth_low = halves(cosine_matrix(depth).T)
    t = tables(rows, lines, depth, wide, narrow)
    width = 3 * LANES
    near = (narrow, wide * count, width)
    far = (wide, narrow * count, width)
    face_rows = (wide * narrow * count, LANES)
    f32 = jnp.float32
    fixed = [jnp.asarray(t[name]) for name in FIXED]
    box_shapes = [
        (lines, depth),
        (depth // LANES, rows * lines, LANES),
        (lines, depth),
        (rows, depth),
        (2, lines, depth),
        (2, rows, depth),
    ]
    shapes = [t["gain"].shape[1:], t["decay"].shape[1:], near, near, far, far, near, far, face_rows, face_rows]
    sems = [len(fixed) + 2, narrow, narrow, wide, wide, narrow, narrow, wide, wide]
    return pl.pallas_call(
        functools.partial(forward_exchange_kernel, steps, groups, wide, narrow),
        grid=(steps + groups,),
        out_shape=[
            jax.ShapeDtypeStruct((lines, rows, depth), f32),
            jax.ShapeDtypeStruct((2, lines, depth), f32),
            jax.ShapeDtypeStruct((2, rows, depth), f32),
            jax.ShapeDtypeStruct((8, depth), f32),
        ],
        in_specs=[slab, slab, slab]
        + table_specs(rows, lines, depth)
        + [IN_HBM] * (len(fixed) + 2)
        + [IN_SMEM],
        out_specs=[
            pl.BlockSpec((GROUP, rows, depth), lambda s: (jnp.maximum(s - steps, 0), 0, 0)),
            whole(2, lines, depth),
            whole(2, rows, depth),
            whole(8, depth),
        ],
        scratch_shapes=[pltpu.VMEM(v, f32) for v in box_shapes]
        + [pltpu.VMEM(v.shape, v.dtype) for v in fixed]
        + [pltpu.VMEM(v, f32) for v in shapes]
        + [pltpu.SemaphoreType.DMA((k,)) for k in sems],
        compiler_params=pltpu.CompilerParams(
            collective_id=0, has_side_effects=True, vmem_limit_bytes=VMEM_LIMIT
        ),
    )(
        first,
        second,
        third,
        jnp.asarray(depth_high),
        jnp.asarray(depth_low),
        jnp.asarray(left_table(cosine_matrix(lines))),
        jnp.asarray(left_table(cosine_matrix(rows))),
        *box_tables(rows, lines, depth),
        *fixed,
        jnp.asarray(t["gain"]),
        jnp.asarray(t["decay"]),
        jnp.asarray(modes(depth), f32),
    )


def inverse(spectrum, wide_flux, narrow_flux, level):
    lines, rows, depth = spectrum.shape
    steps, groups = rows // BLOCK, lines // GROUP
    depth_high, depth_low = halves(cosine_matrix(depth))
    return pl.pallas_call(
        functools.partial(inverse_kernel, groups),
        grid=(steps + groups,),
        out_shape=jax.ShapeDtypeStruct((rows, lines, depth), jnp.float32),
        in_specs=[
            pl.BlockSpec((GROUP, rows, depth), lambda s: (jnp.minimum(s, groups - 1), 0, 0)),
            pl.BlockSpec((2, GROUP, depth), lambda s: (0, jnp.minimum(s, groups - 1), 0)),
            whole(2, rows, depth),
            whole(8, depth),
        ]
        + table_specs(rows, lines, depth),
        out_specs=pl.BlockSpec((BLOCK, lines, depth), lambda s: (jnp.maximum(s - groups, 0), 0, 0)),
        scratch_shapes=[pltpu.VMEM((depth // LANES, rows * lines, LANES), jnp.float32)],
        compiler_params=pltpu.CompilerParams(vmem_limit_bytes=VMEM_LIMIT),
    )(
        spectrum,
        wide_flux,
        narrow_flux,
        level,
        jnp.asarray(depth_high),
        jnp.asarray(depth_low),
        jnp.asarray(left_table(cosine_matrix(lines).T)),
        jnp.asarray(left_table(cosine_matrix(rows).T)),
        *box_tables(rows, lines, depth),
    )


def shards(slope_first, slope_second, slope_third):
    rows, lines, depth = slope_first.shape
    wide = lax.axis_size("wide")
    narrow = lax.axis_size("narrow")
    spectrum, wide_flux, narrow_flux, level = forward_exchange(slope_first, slope_second, slope_third, wide, narrow)
    return inverse(spectrum, wide_flux, narrow_flux, level)


def solution(mesh):
    placed = P("wide", "narrow", None)
    return jax.shard_map(shards, mesh=mesh, in_specs=(placed, placed, placed), out_specs=placed, check_vma=False)
```
